256 devices in a mesh: section: 2 (over x_lo), blk: 128 (over x_hi, y, z, core).
Axes of the slice: x: 4 (x_hi: 2, x_lo: 2; x = x_hi * 2 + x_lo), y: 4, z: 8, core: 2. Of those that a mesh axis runs over, the one named last changes fastest.
Arguments:
- raw_traces: bfloat16 [1024, 8192], P('blk', 'section'), may hold values from -6 to 6
- valid_mask: int32 [1024, 8], P('blk', 'section'), may hold values from 0 to 1, as said below
- block_order: int32 [128], replicated, may hold values from 0 to 127, each once
Outputs:
- correlations: float32 [16, 1024, 256], P('section', 'blk')
The draws below stay inside these ranges and needn't reach their ends.
Inputs may be any that keep to these rules, and one draw needn't show every extreme that they name: `valid_mask`: a station either has no valid segment at all, or each of its segments is valid independently. `block_order`: each block index once.
All inputs are finite; a program needn't handle non-finite values.
Results may differ from the reference program's by a relative error of at most 0.0063.
Values may be sent and summed in bfloat16 or wider, within the bound.
A program may use at most 64 MiB of HBM per device.

```python
import math
import jax
import jax.numpy as jnp
from jax import lax

ST_DEV = 8
L = 1024
NF = 384
BIN_LO = 8
LAGS = 256
TAPS = 33
HW = 50
WF = 32
STEPS = 2
STATIONS = 1024
SEGS = 8
SAMPLES = 8192
NS = 16
RIM = 66
N_BLK = 128


def draw_valid_mask(key, part):
    dead_key = jax.random.fold_in(key, 11)
    each_key = jax.random.fold_in(key, 23)
    alive = jax.random.randint(dead_key, (STATIONS, 1), 0, 16) != 0
    valid = jax.random.randint(each_key, (STATIONS, SEGS), 0, 8) != 0
    return (alive & valid).astype(jnp.int32)


def level_of(own_key, dims, shards, smallest, largest):
    loudness, own = 1.0, jax.random.fold_in(own_key, 6)
    for position, blocks in shards:
        draws = jnp.exp(jax.random.uniform(jax.random.fold_in(own, position), (blocks,), jnp.float32, smallest / len(shards), largest / len(shards)))
        loudness = loudness * jnp.repeat(draws, dims[position] // blocks).reshape([-1 if axis == position else 1 for axis in range(len(dims))])
    return loudness


def normal_values(own_key, extent, scale, most, split=(), kind=jnp.bfloat16):
    entries = jax.random.normal(own_key, extent, jnp.float32) * scale
    if len(split) > 0:
        entries = level_of(own_key, extent, split, -0.22, 0.18) * entries
    return jnp.clip(entries, min=-most, max=most).astype(kind)


def setup_inputs(seed: int = 0) -> dict:
    seeds = jax.random.split(jax.random.key(seed), 4)
    raw_traces = normal_values(seeds[0], (STATIONS, SAMPLES), 1.0, 6.0, ((0, 128), (1, 2)))
    valid_mask = draw_valid_mask(jax.random.fold_in(seeds[3], 71), 0)
    block_order = jax.random.permutation(seeds[2], N_BLK).astype(jnp.int32)
    return {"raw_traces": raw_traces, "valid_mask": valid_mask, "block_order": block_order}


def bandpass_taps():
    offsets = jnp.arange(TAPS, dtype=jnp.float32) - (TAPS - 1) // 2
    low = BIN_LO / L
    high = (BIN_LO + NF) / L
    window = 0.5 + 0.5 * jnp.cos(2.0 * math.pi * offsets / (TAPS + 1))
    return window * (2.0 * high * jnp.sinc(2.0 * high * offsets) - 2.0 * low * jnp.sinc(2.0 * low * offsets))

def filter_normalize(padded):
    taps = bandpass_taps()
    width = padded.shape[1] - (TAPS - 1)
    filtered = taps[0] * padded[:, 0:width]
    for offset in range(1, TAPS):
        filtered = filtered + taps[offset] * padded[:, offset:offset + width]
    magnitude = jnp.abs(filtered)
    window_sum = lax.reduce_window(magnitude, jnp.zeros((), magnitude.dtype), lax.add, (1, 2 * HW + 1), (1, 1), 'VALID')
    centre = filtered[:, HW:HW + window_sum.shape[1]]
    return (centre / (window_sum / (2 * HW + 1) + 1e-06)).astype(jnp.bfloat16)

def forward_table():
    times = jnp.arange(L, dtype=jnp.int32)[:, None]
    bins = BIN_LO + jnp.arange(NF, dtype=jnp.int32)[None, :]
    phase = jnp.mod(times * bins, L).astype(jnp.float32) * (2.0 * math.pi / L)
    return jnp.concatenate([jnp.cos(phase), -jnp.sin(phase)], axis=1).astype(jnp.bfloat16)

def lag_table():
    bins = BIN_LO + jnp.arange(NF, dtype=jnp.int32)[:, None]
    shifts = jnp.arange(LAGS, dtype=jnp.int32)[None, :] - LAGS // 2
    phase = jnp.mod(bins * shifts, L).astype(jnp.float32) * (2.0 * math.pi / L)
    scale = 1.0 / math.sqrt(NF)
    return jnp.concatenate([jnp.cos(phase) * scale, -jnp.sin(phase) * scale], axis=0)

def whiten(normalized, maskvals):
    stations = normalized.shape[0]
    framed = normalized.reshape(-1, L)
    spectra = jnp.dot(framed, forward_table(), preferred_element_type=jnp.float32)
    spectra = spectra.reshape(stations, -1, 2 * NF)
    real_part = spectra[:, :, :NF]
    imag_part = spectra[:, :, NF:]
    amplitude = jnp.sqrt(real_part * real_part + imag_part * imag_part)
    smooth = lax.reduce_window(amplitude, jnp.zeros((), amplitude.dtype), lax.add, (1, 1, 2 * WF + 1), (1, 1, 1), ((0, 0), (0, 0), (WF, WF)))
    factor = maskvals[:, :, None] / (smooth / (2 * WF + 1) + 1e-06)
    return jnp.concatenate([real_part * factor, imag_part * factor], axis=2).astype(jnp.bfloat16)

def cross_lags(sources, receivers):
    source_real = sources[:, :, :NF].astype(jnp.float32)
    source_imag = sources[:, :, NF:].astype(jnp.float32)
    recv_real = receivers[:, :, :NF].astype(jnp.float32)
    recv_imag = receivers[:, :, NF:].astype(jnp.float32)
    real_sum = jnp.einsum('jsf,isf->jif', source_real, recv_real) + jnp.einsum('jsf,isf->jif', source_imag, recv_imag)
    imag_sum = jnp.einsum('jsf,isf->jif', source_real, recv_imag) - jnp.einsum('jsf,isf->jif', source_imag, recv_real)
    stacked = jnp.concatenate([real_sum, imag_sum], axis=2)
    count_src, count_rec = (stacked.shape[0], stacked.shape[1])
    lagged = jnp.dot(stacked.reshape(count_src * count_rec, 2 * NF), lag_table(), precision=lax.Precision.HIGHEST)
    return lagged.reshape(count_src, count_rec, LAGS)

def reference(raw_traces, valid_mask, block_order):
    padded = jnp.pad(raw_traces.astype(jnp.float32), ((0, 0), (RIM, RIM)))
    normalized = filter_normalize(padded)
    maskvals = valid_mask.astype(jnp.float32)
    whitened = whiten(normalized, maskvals)

    def one_block(owner):
        start = (owner * ST_DEV).astype(jnp.int32)
        sources = lax.dynamic_slice_in_dim(whitened, start, ST_DEV, 0)
        source_mask = lax.dynamic_slice_in_dim(maskvals, start, ST_DEV, 0)
        counts = jnp.dot(source_mask, maskvals.T, precision=lax.Precision.HIGHEST)
        return cross_lags(sources, whitened) / jnp.maximum(counts, 1.0)[:, :, None]
    blocks = lax.map(one_block, block_order[:STEPS])
    return blocks.reshape(NS, STATIONS, LAGS)
```

```python
import functools
import math

import jax
import jax.numpy as jnp
import ml_dtypes
import numpy as np
from jax import lax
from jax.experimental import pallas as pl
from jax.experimental.pallas import tpu as pltpu
from jax.sharding import PartitionSpec as P

L = 1024
NF = 384
BIN_LO = 8
LAGS = 256
TAPS = 33
HW = 50
WF = 32
NT = 32
KT = NF // 128
SEG = 4
ST = 8
PIECES = SEG * KT + 1
PLANE = 16
DEPTH = 8
MESH = pl.DeviceIdType.MESH
f32 = jnp.float32
bf16 = jnp.bfloat16


def split(values):
    high = values.astype(np.float32).astype(ml_dtypes.bfloat16)
    low = (values - high.astype(np.float64)).astype(ml_dtypes.bfloat16)
    return high, low


def tables():
    half = (TAPS - 1) // 2
    k = np.arange(-half, half + 1).astype(np.float64)
    a, b = BIN_LO / L, (BIN_LO + NF) / L
    taps = (0.5 + 0.5 * np.cos(2 * np.pi * k / (TAPS + 1))) * (
        2 * b * np.sinc(2 * b * k) - 2 * a * np.sinc(2 * a * k)
    )
    shift = np.arange(128)[None, :] + 128 - np.arange(384)[:, None]
    band = np.where(np.abs(shift) <= half, taps[np.clip(shift + half, 0, TAPS - 1)], 0.0)
    fir = np.concatenate(split(band), axis=1)
    box = (np.abs(shift) <= HW).astype(ml_dtypes.bfloat16)
    box = np.concatenate([box, box], axis=0)
    bins = BIN_LO + np.arange(NF)
    phase = (np.arange(L)[:, None] * bins[None, :]) % L * (2 * np.pi / L)
    dft = np.concatenate([np.cos(phase), -np.sin(phase)], axis=1)
    dft = dft.astype(np.float32).astype(ml_dtypes.bfloat16)
    near = np.abs(np.arange(NF)[:, None] - np.arange(NF)[None, :]) <= WF
    near = near.astype(ml_dtypes.bfloat16)
    phase = (bins[:, None] * (np.arange(LAGS) - LAGS // 2)[None, :]) % L * (2 * np.pi / L)
    lag = np.concatenate([np.cos(phase), -np.sin(phase)], axis=0) / math.sqrt(NF)
    lag = np.concatenate(split(lag), axis=1)
    return fir, box, dft, near, lag


def dot(a, b):
    return jnp.dot(a, b, preferred_element_type=f32)


def halves(x):
    high = x.astype(bf16)
    return high, (x - high.astype(f32)).astype(bf16)


def normalize(tiles, fir, box):
    zero = jnp.zeros((ST, 128), f32)
    left = jnp.concatenate([zero] + tiles[:-1], axis=0).astype(bf16)
    mid = jnp.concatenate(tiles, axis=0).astype(bf16)
    right = jnp.concatenate(tiles[1:] + [zero], axis=0).astype(bf16)
    both = dot(jnp.concatenate([left, mid, right], axis=1), fir)
    filtered = both[:, :128] + both[:, 128:]
    size = jnp.abs(filtered)
    rows = NT * ST
    parts = [halves(size[ST * i : ST * i + rows]) for i in range(3)]
    window = dot(jnp.concatenate([p[0] for p in parts] + [p[1] for p in parts], axis=1), box)
    return filtered[ST : ST + rows] / (window * (1.0 / (2 * HW + 1)) + 1e-06)


def spectra_of(normalized, dft, near, mask):
    per = L // 128
    lanes = [
        jnp.concatenate(
            [normalized[(g * per + t) * ST : (g * per + t + 1) * ST] for g in range(SEG)], axis=0
        )
        for t in range(per)
    ]
    spectra = dot(jnp.concatenate(lanes, axis=1).astype(bf16), dft)
    re, im = spectra[:, :NF], spectra[:, NF:]
    high, low = halves(jnp.sqrt(re * re + im * im))
    smooth = dot(high, near) + dot(low, near)
    factor = mask / (smooth * (1.0 / (2 * WF + 1)) + 1e-06)
    return re * factor, im * factor


def kernel(
    raw_ref, mask_ref, order_ref, fir_hbm, box_hbm, dft_hbm, near_hbm, lag_hbm, out_ref,
    fir_ref, box_ref, dft_ref, near_ref, lag_ref,
    halo, wfull, slots1, cand, slots2, picked, slots3, stack,
    table_sem, halo_sem, pair_sem, one_sem, two_sem, three_sem,
):
    half = lax.axis_index("section")
    blk = lax.axis_index("blk")
    me = (blk // 16) * 2 + blk % 2
    z = (blk // 2) % DEPTH
    collects = me < PIECES

    def device(section, plane, depth):
        return (section, (plane // 2) * 16 + depth * 2 + plane % 2)

    def remote(src, dst, sems, to):
        return pltpu.make_async_remote_copy(
            src_ref=src, dst_ref=dst, send_sem=sems.at[0], recv_sem=sems.at[1],
            device_id=to, device_id_type=MESH,
        )

    def wait(ref, sem):
        pltpu.make_async_copy(ref, ref, sem).wait()

    copies = [
        pltpu.make_async_copy(src, dst, table_sem.at[i])
        for i, (src, dst) in enumerate(
            (
                (fir_hbm, fir_ref), (box_hbm, box_ref), (dft_hbm, dft_ref),
                (near_hbm, near_ref), (lag_hbm, lag_ref),
            )
        )
    ]
    for copy in copies:
        copy.start()

    mates = [lax.rem(me + i, PLANE) for i in range(1, PLANE)]
    column = [(i // DEPTH, i % DEPTH) for i in range(1, 2 * DEPTH)]
    column = [(lax.rem(half + i, 2), lax.rem(z + j, DEPTH)) for i, j in column]

    barrier = pltpu.get_barrier_semaphore()
    for mate in mates:
        pl.semaphore_signal(barrier, inc=1, device_id=device(half, mate, z), device_id_type=MESH)
    for section, depth in column:
        pl.semaphore_signal(
            barrier, inc=1, device_id=device(section, me, depth), device_id_type=MESH
        )
    pl.semaphore_wait(barrier, len(mates) + len(column))

    other = device(1 - half, me, z)
    edge = pl.multiple_of((1 - half) * ((NT - 1) * 128), 128)
    send_halo = remote(raw_ref.at[:, pl.ds(edge, 128)], halo, halo_sem, other)
    send_halo.start()
    raw = raw_ref[...].astype(f32)
    send_halo.wait()
    beyond = halo[...].astype(f32)
    tiles = [raw[:, 128 * i : 128 * (i + 1)] for i in range(NT)]
    before = jnp.where(half == 1, beyond, 0.0)
    after = jnp.where(half == 0, beyond, 0.0)
    copies[0].wait()
    copies[1].wait()
    normalized = normalize([before] + tiles + [after], fir_ref[...], box_ref[...])
    mask = mask_ref[...].astype(f32)
    column_mask = jnp.concatenate([mask[:, g : g + 1] for g in range(SEG)], axis=0)
    copies[2].wait()
    copies[3].wait()
    re, im = spectra_of(normalized, dft_ref[...], near_ref[...], column_mask)
    for g in range(SEG):
        for k in range(KT):
            place = (slice(ST * g, ST * (g + 1)), slice(128 * k, 128 * (k + 1)))
            piece = jnp.concatenate([re[place], im[place]], axis=0)
            wfull[half, g * KT + k] = piece.astype(bf16)
    lane = lax.broadcasted_iota(jnp.int32, (ST, 128), 1)
    flags = jnp.zeros((ST, 128), f32)
    for g in range(SEG):
        flags = jnp.where(lane == g, mask[:, g : g + 1], flags)
    wfull[half, PIECES - 1] = jnp.concatenate([flags, flags], axis=0).astype(bf16)

    for mate in mates:

        @pl.when(mate < PIECES)
        def _(mate=mate):
            remote(
                wfull.at[half, mate], slots1.at[me], one_sem, device(half, mate, z)
            ).start()

    pair = remote(wfull.at[half], wfull.at[half], pair_sem, other)
    pair.start()

    root = [order_ref[i] for i in range(2)]
    root_plane = [(r // 16) * 2 + r % 2 for r in root]
    mine = jnp.where(half == 0, root[0], root[1])
    mine_z = (mine // 2) % DEPTH

    @pl.when(collects)
    def _():
        slots1[me] = wfull[half, me]
        wait(slots1.at[pl.ds(0, PLANE - 1)], one_sem.at[1])
        for i in range(2):
            cand[i] = slots1[root_plane[i]]
        for section, depth in column:
            remote(
                cand.at[section], slots2.at[half, z], two_sem, device(section, me, depth)
            ).start()
        slots2[half, z] = cand[half]
        wait(slots1.at[pl.ds(0, PLANE - 1)], two_sem.at[1])
        for i in range(2):
            picked[i] = slots2[i, mine_z]
        for mate in mates:
            remote(picked, slots3.at[me], three_sem, device(half, mate, z)).start()
        for i in range(2):
            slots3[me, i] = picked[i]

    pair.wait()
    copies[4].wait()

    @pl.when(collects)
    def _():
        wait(slots3.at[pl.ds(0, PIECES - 1)], three_sem.at[1])

    @pl.when(jnp.logical_not(collects))
    def _():
        wait(slots3.at[pl.ds(0, PIECES)], three_sem.at[1])

    for k in range(KT):
        real = [jnp.zeros((ST, 128), f32)] * ST
        imag = [jnp.zeros((ST, 128), f32)] * ST
        for i in range(2):
            for g in range(SEG):
                station = wfull[i, g * KT + k].astype(f32)
                source = slots3[g * KT + k, i].astype(f32)
                re_s, im_s = station[:ST], station[ST:]
                for n in range(ST):
                    re_n = source[n : n + 1]
                    im_n = source[ST + n : ST + n + 1]
                    real[n] = real[n] + (re_s * re_n + im_s * im_n)
                    imag[n] = imag[n] + (im_s * re_n - re_s * im_n)
        for n in range(ST):
            stack[ST * n : ST * (n + 1), 128 * k : 128 * (k + 1)] = real[n]
            stack[ST * n : ST * (n + 1), NF + 128 * k : NF + 128 * (k + 1)] = imag[n]
    high, low = halves(stack[...])
    first = dot(high, lag_ref[...])
    lagged = first[:, :LAGS] + first[:, LAGS:] + dot(low, lag_ref[:, :LAGS])
    own = [wfull[i, PIECES - 1].astype(f32)[:ST] for i in range(2)]
    theirs = [slots3[PIECES - 1, i].astype(f32)[:ST] for i in range(2)]
    for n in range(ST):
        count = own[0] * theirs[0][n : n + 1] + own[1] * theirs[1][n : n + 1]
        count = jnp.maximum(jnp.sum(count, axis=1, keepdims=True), 1.0)
        out_ref[n] = lagged[ST * n : ST * (n + 1)] / count

    @pl.when(jnp.logical_not(collects))
    def _():
        wait(slots1.at[pl.ds(0, PIECES)], one_sem.at[0])

    @pl.when(collects)
    def _():
        wait(slots1.at[pl.ds(0, PIECES - 1)], one_sem.at[0])
        wait(slots1.at[pl.ds(0, PLANE - 1)], two_sem.at[0])
        wait(slots3.at[pl.ds(0, PLANE - 1)], three_sem.at[0])


def shards(raw_traces, valid_mask, block_order):
    constants = [jnp.asarray(t) for t in tables()]
    vmem = pl.BlockSpec(memory_space=pltpu.VMEM)
    piece = (2 * ST, 128)
    pair = pltpu.SemaphoreType.DMA((2,))
    return pl.pallas_call(
        kernel,
        out_shape=jax.ShapeDtypeStruct((ST, ST, LAGS), f32),
        in_specs=[vmem, vmem, pl.BlockSpec(memory_space=pltpu.SMEM)]
        + [pl.BlockSpec(memory_space=pl.ANY)] * len(constants),
        out_specs=vmem,
        scratch_shapes=[pltpu.VMEM(c.shape, c.dtype) for c in constants]
        + [
            pltpu.VMEM((ST, 128), bf16),
            pltpu.VMEM((2, PIECES) + piece, bf16),
            pltpu.VMEM((PLANE,) + piece, bf16),
            pltpu.VMEM((2,) + piece, bf16),
            pltpu.VMEM((2, DEPTH) + piece, bf16),
            pltpu.VMEM((2,) + piece, bf16),
            pltpu.VMEM((PLANE, 2) + piece, bf16),
            pltpu.VMEM((ST * ST, 2 * NF), f32),
            pltpu.SemaphoreType.DMA((len(constants),)),
            pair, pair, pair, pair, pair,
        ],
        compiler_params=pltpu.CompilerParams(
            collective_id=0, has_side_effects=True, vmem_limit_bytes=48 << 20
        ),
    )(raw_traces, valid_mask, block_order, *constants)


def solution(mesh):
    return jax.shard_map(
        shards,
        mesh=mesh,
        in_specs=(P("blk", "section"), P("blk", "section"), P()),
        out_specs=P("section", "blk", None),
        check_vma=False,
    )
```

```python
import math

import jax
import jax.numpy as jnp
import ml_dtypes
import numpy as np
from jax import lax
from jax.experimental import pallas as pl
from jax.experimental.pallas import tpu as pltpu
from jax.sharding import PartitionSpec as P

L = 1024
NF = 384
BIN_LO = 8
LAGS = 256
TAPS = 33
HW = 50
WF = 32
KT = NF // 128
SEGS = 8
SEG = 4
HALF = SEG * L
ST = 8
PIECE = 256
VMEM_KIB = 61920
PLANE = 16
DEPTH = 8
MESH = pl.DeviceIdType.MESH
f32 = jnp.float32
bf16 = jnp.bfloat16


def split(values):
    high = values.astype(np.float32).astype(ml_dtypes.bfloat16)
    low = (values - high.astype(np.float64)).astype(ml_dtypes.bfloat16)
    return high, low


def tables():
    half = (TAPS - 1) // 2
    k = np.arange(-half, half + 1).astype(np.float64)
    a, b = BIN_LO / L, (BIN_LO + NF) / L
    taps = (0.5 + 0.5 * np.cos(2 * np.pi * k / (TAPS + 1))) * (
        2 * b * np.sinc(2 * b * k) - 2 * a * np.sinc(2 * a * k)
    )
    shift = np.arange(128)[None, :] + 128 - np.arange(384)[:, None]
    band = np.where(np.abs(shift) <= half, taps[np.clip(shift + half, 0, TAPS - 1)], 0.0)
    fir = np.concatenate(split(band), axis=1)
    box = (np.abs(shift) <= HW).astype(ml_dtypes.bfloat16)
    box = np.concatenate([box, box], axis=0)
    bins = BIN_LO + np.arange(NF)
    phase = (np.arange(L)[:, None] * bins[None, :]) % L * (2 * np.pi / L)
    dft = np.concatenate([np.cos(phase), -np.sin(phase)], axis=1)
    dft = dft.astype(np.float32).astype(ml_dtypes.bfloat16)
    near = np.abs(np.arange(NF)[:, None] - np.arange(NF)[None, :]) <= WF
    near = near.astype(ml_dtypes.bfloat16)
    phase = (bins[:, None] * (np.arange(LAGS) - LAGS // 2)[None, :]) % L * (2 * np.pi / L)
    lag = np.concatenate([np.cos(phase), -np.sin(phase)], axis=0) / math.sqrt(NF)
    lag = np.concatenate(split(lag), axis=1)
    return fir, box, dft, near, lag


def dot(a, b):
    return jnp.dot(a, b, preferred_element_type=f32)


def halves(x):
    high = x.astype(bf16)
    return high, (x - high.astype(f32)).astype(bf16)


def whiten(tiles, masks, fir, box, dft, near):
    count = len(tiles)
    zero = jnp.zeros((ST, 128), f32)
    left = jnp.concatenate([zero, zero] + tiles, axis=0).astype(bf16)
    mid = jnp.concatenate([zero] + tiles + [zero], axis=0).astype(bf16)
    right = jnp.concatenate(tiles + [zero, zero], axis=0).astype(bf16)
    both = dot(jnp.concatenate([left, mid, right], axis=1), fir)
    filtered = both[:, :128] + both[:, 128:]
    size = jnp.abs(filtered)
    rows = count * ST
    parts = [halves(size[ST * i : ST * i + rows]) for i in range(3)]
    window = dot(jnp.concatenate([p[0] for p in parts] + [p[1] for p in parts], axis=1), box)
    normalized = filtered[ST : ST + rows] / (window * (1.0 / (2 * HW + 1)) + 1e-06)
    per = L // 128
    lanes = [
        jnp.concatenate(
            [normalized[(g * per + t) * ST : (g * per + t + 1) * ST] for g in range(SEGS)], axis=0
        )
        for t in range(per)
    ]
    spectra = dot(jnp.concatenate(lanes, axis=1).astype(bf16), dft)
    re, im = spectra[:, :NF], spectra[:, NF:]
    high, low = halves(jnp.sqrt(re * re + im * im))
    smooth = dot(high, near) + dot(low, near)
    factor = jnp.concatenate(masks, axis=0) / (smooth * (1.0 / (2 * WF + 1)) + 1e-06)
    return (re * factor).astype(bf16).astype(f32), (im * factor).astype(bf16).astype(f32)


def hour(ref):
    return [ref[:, 128 * i : 128 * (i + 1)].astype(f32) for i in range(SEGS * L // 128)]


def kernel(
    raw_hbm, mask_hbm, order_hbm, fir_hbm, box_hbm, dft_hbm, near_hbm, lag_hbm, out_ref,
    mask_ref, order_ref, fir_ref, box_ref, dft_ref, near_ref, lag_ref,
    own, own_mask, slots1, cand, slots2, picked, source,
    mslots1, mcand, mslots2, mpicked, source_mask, station, stack,
    copy_sem, pair_sem, mpair_sem, one_sem, two_sem, three_sem, mone_sem, mtwo_sem, mthree_sem,
):
    half = lax.axis_index("section")
    blk = lax.axis_index("blk")
    me = (blk // 16) * 2 + blk % 2
    z = (blk // 2) % DEPTH

    def device(section, plane, depth):
        return (section, (plane // 2) * 16 + depth * 2 + plane % 2)

    def remote(src, dst, sems, to):
        return pltpu.make_async_remote_copy(
            src_ref=src, dst_ref=dst, send_sem=sems.at[0], recv_sem=sems.at[1],
            device_id=to, device_id_type=MESH,
        )

    def wait(ref, sem):
        pltpu.make_async_copy(ref, ref, sem).wait()

    def lanes(start, size):
        return pl.ds(pl.multiple_of(start, 128), size)

    mine = own.at[:, lanes(half * HALF, HALF)]
    copies = [
        pltpu.make_async_copy(src, dst, copy_sem.at[i])
        for i, (src, dst) in enumerate(
            (
                (raw_hbm, mine), (mask_hbm, mask_ref), (order_hbm, order_ref),
                (fir_hbm, fir_ref), (box_hbm, box_ref), (dft_hbm, dft_ref),
                (near_hbm, near_ref), (lag_hbm, lag_ref),
            )
        )
    ]
    for copy in copies:
        copy.start()

    mates = [lax.rem(me + i, PLANE) for i in range(1, PLANE)]
    both = [(lax.rem(half + i, 2), lax.rem(me + j, PLANE)) for i in range(2) for j in range(PLANE)]
    both = both[1:]
    column = [lax.rem(z + i, DEPTH) for i in range(1, DEPTH)]

    barrier = pltpu.get_barrier_semaphore()
    for section, mate in both:
        pl.semaphore_signal(
            barrier, inc=1, device_id=device(section, mate, z), device_id_type=MESH
        )
    for depth in column:
        pl.semaphore_signal(barrier, inc=1, device_id=device(half, me, depth), device_id_type=MESH)

    copies[1].wait()
    flags = mask_ref[...].astype(f32)
    eye = lax.broadcasted_iota(jnp.int32, (ST, ST), 0) == lax.broadcasted_iota(
        jnp.int32, (ST, ST), 1
    )
    lane = lax.broadcasted_iota(jnp.int32, (ST, 128), 1)
    tile = jnp.zeros((ST, 128), f32)
    for g in range(SEG):
        row = jnp.where(eye, jnp.broadcast_to(flags[g : g + 1], (ST, ST)), 0.0)
        tile = jnp.where(lane == g, jnp.sum(row, axis=1, keepdims=True), tile)
    own_mask[half] = tile.astype(bf16)
    copies[0].wait()
    pl.semaphore_wait(barrier, len(both) + len(column))

    def piece(q):
        return own.at[:, lanes(half * HALF + q * PIECE, PIECE)]

    for mate in mates:
        remote(piece(mate), slots1.at[me], one_sem, device(half, mate, z)).start()

    @pl.when(me != 0)
    def _():
        remote(own_mask.at[half], mslots1.at[me], mone_sem, device(half, 0, z)).start()

    other = device(1 - half, me, z)
    pair = [
        remote(mine, mine, pair_sem, other),
        remote(own_mask.at[half], own_mask.at[half], mpair_sem, other),
    ]
    for copy in pair:
        copy.start()
    slots1[me] = own[:, lanes(half * HALF + me * PIECE, PIECE)]
    copies[2].wait()
    root = [order_ref[i] for i in range(2)]
    root_plane = [(r // 16) * 2 + r % 2 for r in root]
    root_z = [(r // 2) % DEPTH for r in root]

    wait(slots1.at[pl.ds(0, PLANE - 1)], one_sem.at[1])
    for i in range(2):
        cand[i] = slots1[root_plane[i]]
    for depth in column:
        remote(cand, slots2.at[z], two_sem, device(half, me, depth)).start()
    slots2[z] = cand[...]

    @pl.when(me == 0)
    def _():
        mslots1[0] = own_mask[half]
        wait(mslots1.at[pl.ds(0, PLANE - 1)], mone_sem.at[1])
        for i in range(2):
            mcand[i] = mslots1[root_plane[i]]
        for depth in column:
            remote(mcand, mslots2.at[z], mtwo_sem, device(half, me, depth)).start()
        mslots2[z] = mcand[...]

    for copy in pair:
        copy.wait()
    for i in range(3, 7):
        copies[i].wait()
    weights = (fir_ref, box_ref, dft_ref, near_ref)
    masks = [own_mask[i].astype(f32) for i in range(2)]
    columns = [m[:, g : g + 1] for m in masks for g in range(SEG)]
    station[0], station[1] = whiten(hour(own), columns, *[w[...] for w in weights])

    wait(slots2.at[pl.ds(0, DEPTH - 1)], two_sem.at[1])
    for i in range(2):
        picked[i] = slots2[root_z[i], i]
    place = lanes(half * HALF + me * PIECE, PIECE)
    for section, mate in both:
        remote(
            picked.at[section], source.at[:, place], three_sem, device(section, mate, z)
        ).start()
    source[:, place] = picked[half]

    @pl.when(me == 0)
    def _():
        wait(mslots2.at[pl.ds(0, DEPTH - 1)], mtwo_sem.at[1])
        for i in range(2):
            mpicked[i] = mslots2[root_z[i], i]
        for section, mate in both:
            remote(
                mpicked.at[section], source_mask.at[half], mthree_sem, device(section, mate, z)
            ).start()
        source_mask[half] = mpicked[half]

    copies[7].wait()
    wait(source.at[:, pl.ds(0, 31 * PIECE)], three_sem.at[1])

    @pl.when(me == 0)
    def _():
        wait(source_mask.at[0], mthree_sem.at[1])

    @pl.when(me != 0)
    def _():
        wait(source_mask, mthree_sem.at[1])

    theirs = [source_mask[i].astype(f32) for i in range(2)]
    columns = [m[:, g : g + 1] for m in theirs for g in range(SEG)]
    source_re, source_im = whiten(hour(source), columns, *[w[...] for w in weights])
    for k in range(KT):
        part = slice(128 * k, 128 * (k + 1))
        real = [jnp.zeros((ST, 128), f32)] * ST
        imag = [jnp.zeros((ST, 128), f32)] * ST
        for g in range(SEGS):
            re_s = station[0, ST * g : ST * (g + 1), part]
            im_s = station[1, ST * g : ST * (g + 1), part]
            for n in range(ST):
                re_n = source_re[ST * g + n : ST * g + n + 1, part]
                im_n = source_im[ST * g + n : ST * g + n + 1, part]
                real[n] = real[n] + (re_s * re_n + im_s * im_n)
                imag[n] = imag[n] + (im_s * re_n - re_s * im_n)
        for n in range(ST):
            stack[ST * n : ST * (n + 1), 128 * k : 128 * (k + 1)] = real[n]
            stack[ST * n : ST * (n + 1), NF + 128 * k : NF + 128 * (k + 1)] = imag[n]
    high, low = halves(stack[...])
    first = dot(high, lag_ref[...])
    lagged = first[:, :LAGS] + first[:, LAGS:] + dot(low, lag_ref[:, :LAGS])
    for n in range(ST):
        count = masks[0] * theirs[0][n : n + 1] + masks[1] * theirs[1][n : n + 1]
        count = jnp.maximum(jnp.sum(count, axis=1, keepdims=True), 1.0)
        out_ref[n] = lagged[ST * n : ST * (n + 1)] / count

    wait(slots1.at[pl.ds(0, PLANE - 1)], one_sem.at[0])
    wait(slots2.at[pl.ds(0, DEPTH - 1)], two_sem.at[0])
    wait(source.at[:, pl.ds(0, 31 * PIECE)], three_sem.at[0])

    @pl.when(me == 0)
    def _():
        wait(mslots2.at[pl.ds(0, DEPTH - 1)], mtwo_sem.at[0])
        wait(source.at[:, pl.ds(0, 31 * 128)], mthree_sem.at[0])

    @pl.when(me != 0)
    def _():
        wait(mslots1.at[0], mone_sem.at[0])


def shards(raw_traces, valid_mask, block_order):
    constants = [jnp.asarray(t) for t in tables()]
    hbm = pl.BlockSpec(memory_space=pl.ANY)
    wide = (ST, PIECE)
    flag = (ST, 128)
    pair = pltpu.SemaphoreType.DMA((2,))
    return pl.pallas_call(
        kernel,
        out_shape=jax.ShapeDtypeStruct((ST, ST, LAGS), f32),
        in_specs=[hbm] * (3 + len(constants)),
        out_specs=pl.BlockSpec(memory_space=pltpu.VMEM),
        scratch_shapes=[
            pltpu.VMEM((SEG, ST), jnp.int32),
            pltpu.SMEM(block_order.shape, jnp.int32),
        ]
        + [pltpu.VMEM(c.shape, c.dtype) for c in constants]
        + [
            pltpu.VMEM((ST, 2 * HALF), bf16),
            pltpu.VMEM((2,) + flag, bf16),
            pltpu.VMEM((PLANE,) + wide, bf16),
            pltpu.VMEM((2,) + wide, bf16),
            pltpu.VMEM((DEPTH, 2) + wide, bf16),
            pltpu.VMEM((2,) + wide, bf16),
            pltpu.VMEM((ST, 2 * HALF), bf16),
            pltpu.VMEM((PLANE,) + flag, bf16),
            pltpu.VMEM((2,) + flag, bf16),
            pltpu.VMEM((DEPTH, 2) + flag, bf16),
            pltpu.VMEM((2,) + flag, bf16),
            pltpu.VMEM((2,) + flag, bf16),
            pltpu.VMEM((2, SEGS * ST, NF), f32),
            pltpu.VMEM((ST * ST, 2 * NF), f32),
            pltpu.SemaphoreType.DMA((3 + len(constants),)),
            pair, pair, pair, pair, pair, pair, pair, pair,
        ],
        compiler_params=pltpu.CompilerParams(
            collective_id=0, has_side_effects=True, vmem_limit_bytes=VMEM_KIB << 10
        ),
    )(raw_traces, valid_mask.T, block_order, *constants)


def solution(mesh):
    return jax.shard_map(
        shards,
        mesh=mesh,
        in_specs=(P("blk", "section"), P("blk", "section"), P()),
        out_specs=P("section", "blk", None),
        check_vma=False,
    )
```

```python
import math

import jax
import jax.numpy as jnp
import ml_dtypes
import numpy as np
from jax import lax
from jax.experimental import pallas as pl
from jax.experimental.pallas import tpu as pltpu
from jax.sharding import PartitionSpec as P

L = 1024
NF = 384
BIN_LO = 8
LAGS = 256
TAPS = 33
HW = 50
WF = 32
KT = NF // 128
SEGS = 8
SEG = 4
HALF = SEG * L
ST = 8
PIECE = 256
VMEM_KIB = 32768
PLANE = 16
COLUMNS = 8
DEPTH = 8
N_BLK = 128
MESH = pl.DeviceIdType.MESH
f32 = jnp.float32
bf16 = jnp.bfloat16


def split(values):
    high = values.astype(np.float32).astype(ml_dtypes.bfloat16)
    low = (values - high.astype(np.float64)).astype(ml_dtypes.bfloat16)
    return high, low


def tables():
    half = (TAPS - 1) // 2
    k = np.arange(-half, half + 1).astype(np.float64)
    a, b = BIN_LO / L, (BIN_LO + NF) / L
    taps = (0.5 + 0.5 * np.cos(2 * np.pi * k / (TAPS + 1))) * (
        2 * b * np.sinc(2 * b * k) - 2 * a * np.sinc(2 * a * k)
    )
    shift = np.arange(128)[None, :] + 128 - np.arange(384)[:, None]
    band = np.where(np.abs(shift) <= half, taps[np.clip(shift + half, 0, TAPS - 1)], 0.0)
    fir = np.concatenate(split(band), axis=1)
    box = (np.abs(shift) <= HW).astype(ml_dtypes.bfloat16)
    box = np.concatenate([box, box], axis=0)
    bins = BIN_LO + np.arange(NF)
    phase = (np.arange(L)[:, None] * bins[None, :]) % L * (2 * np.pi / L)
    dft = np.concatenate([np.cos(phase), -np.sin(phase)], axis=1)
    dft = dft.astype(np.float32).astype(ml_dtypes.bfloat16)
    near = np.abs(np.arange(NF)[:, None] - np.arange(NF)[None, :]) <= WF
    near = near.astype(ml_dtypes.bfloat16)
    phase = (bins[:, None] * (np.arange(LAGS) - LAGS // 2)[None, :]) % L * (2 * np.pi / L)
    lag = np.concatenate([np.cos(phase), -np.sin(phase)], axis=0) / math.sqrt(NF)
    lag = np.concatenate(split(lag), axis=1)
    return fir, box, dft, near, lag


def dot(a, b):
    return jnp.dot(a, b, preferred_element_type=f32)


def halves(x):
    high = x.astype(bf16)
    return high, (x - high.astype(f32)).astype(bf16)


def whiten(tiles, masks, fir, box, dft, near):
    count = len(tiles)
    zero = jnp.zeros((ST, 128), f32)
    left = jnp.concatenate([zero, zero] + tiles, axis=0).astype(bf16)
    mid = jnp.concatenate([zero] + tiles + [zero], axis=0).astype(bf16)
    right = jnp.concatenate(tiles + [zero, zero], axis=0).astype(bf16)
    both = dot(jnp.concatenate([left, mid, right], axis=1), fir)
    filtered = both[:, :128] + both[:, 128:]
    size = jnp.abs(filtered)
    rows = count * ST
    parts = [halves(size[ST * i : ST * i + rows]) for i in range(3)]
    window = dot(jnp.concatenate([p[0] for p in parts] + [p[1] for p in parts], axis=1), box)
    normalized = filtered[ST : ST + rows] / (window * (1.0 / (2 * HW + 1)) + 1e-06)
    per = L // 128
    lanes = [
        jnp.concatenate(
            [normalized[(g * per + t) * ST : (g * per + t + 1) * ST] for g in range(SEGS)], axis=0
        )
        for t in range(per)
    ]
    spectra = dot(jnp.concatenate(lanes, axis=1).astype(bf16), dft)
    re, im = spectra[:, :NF], spectra[:, NF:]
    high, low = halves(jnp.sqrt(re * re + im * im))
    smooth = dot(high, near) + dot(low, near)
    factor = jnp.concatenate(masks, axis=0) / (smooth * (1.0 / (2 * WF + 1)) + 1e-06)
    return (re * factor).astype(bf16).astype(f32), (im * factor).astype(bf16).astype(f32)


def hour(ref):
    return [ref[h, :, 128 * i : 128 * (i + 1)].astype(f32) for h in range(2) for i in range(HALF // 128)]


def kernel(
    raw_hbm, mask_hbm, order_hbm, fir_hbm, box_hbm, dft_hbm, near_hbm, lag_hbm, out_ref,
    mask_ref, order_ref, fir_ref, box_ref, dft_ref, near_ref, lag_ref,
    own, own_mask, slots1, cand, slots2, picked, source, bulk,
    mslots1, mcand, mslots2, mpicked, source_mask, station, stack,
    copy_sem, pair_sem, mpair_sem, one_sem, two_sem, three_sem, mone_sem, mtwo_sem, mthree_sem,
):
    half = lax.axis_index("section")
    blk = lax.axis_index("blk")
    me = (blk // 16) * 2 + blk % 2
    z = (blk // 2) % DEPTH
    collects = me < COLUMNS
    late = me >= COLUMNS
    slot = half * COLUMNS + me % COLUMNS
    keeps_masks = half * N_BLK + blk == z * 2

    def device(section, plane, depth):
        return (section, (plane // 2) * 16 + depth * 2 + plane % 2)

    def collector(q):
        return device(q // COLUMNS, q % COLUMNS, z)

    def remote(src, dst, sems, to):
        return pltpu.make_async_remote_copy(
            src_ref=src, dst_ref=dst, send_sem=sems.at[0], recv_sem=sems.at[1],
            device_id=to, device_id_type=MESH,
        )

    def wait(ref, sem):
        pltpu.make_async_copy(ref, ref, sem).wait()

    def lanes(q):
        return pl.ds(pl.multiple_of(q * PIECE, PIECE), PIECE)

    mates = [lax.rem(slot + i, PLANE) for i in range(1, PLANE)]
    column = [lax.rem(z + i, DEPTH) for i in range(1, DEPTH)]
    rest = [(i, COLUMNS + j) for j in range(COLUMNS) for i in range(2)]
    other = device(1 - half, me, z)
    barrier = pltpu.get_barrier_semaphore()

    def signal(to):
        pl.semaphore_signal(barrier, inc=1, device_id=to, device_id_type=MESH)

    @pl.when(collects)
    def _():
        for depth in column:
            signal(device(half, me, depth))
        for mate in mates:
            signal(collector(mate))
        for section, plane in rest:
            signal(device(section, plane, z))

    @pl.when(late)
    def _():
        signal(other)

    mine = own.at[half]
    copies = [
        pltpu.make_async_copy(src, dst, copy_sem.at[i])
        for i, (src, dst) in enumerate(
            (
                (raw_hbm, mine), (mask_hbm, mask_ref), (order_hbm, order_ref),
                (fir_hbm, fir_ref), (box_hbm, box_ref), (dft_hbm, dft_ref),
                (near_hbm, near_ref), (lag_hbm, lag_ref),
            )
        )
    ]
    for copy in copies:
        copy.start()
    copies[1].wait()
    flags = mask_ref[...].astype(f32)
    eye = lax.broadcasted_iota(jnp.int32, (ST, ST), 0) == lax.broadcasted_iota(
        jnp.int32, (ST, ST), 1
    )
    lane = lax.broadcasted_iota(jnp.int32, (ST, 128), 1)
    tile = jnp.zeros((ST, 128), f32)
    for g in range(SEG):
        row = jnp.where(eye, jnp.broadcast_to(flags[g : g + 1], (ST, ST)), 0.0)
        tile = jnp.where(lane == g, jnp.sum(row, axis=1, keepdims=True), tile)
    own_mask[half] = tile.astype(bf16)
    copies[0].wait()

    @pl.when(collects)
    def _():
        pl.semaphore_wait(barrier, len(column) + len(mates))

    @pl.when(late)
    def _():
        pl.semaphore_wait(barrier, PLANE + 1)

    def piece(q):
        return remote(own.at[half, :, lanes(q)], slots1.at[half, me], one_sem, collector(q))

    for mate in mates:
        piece(mate).start()

    @pl.when(late)
    def _():
        piece(slot).start()

    pair = [
        remote(mine, mine, pair_sem, other),
        remote(own_mask.at[half], own_mask.at[half], mpair_sem, other),
    ]
    for copy in pair:
        copy.start()

    @pl.when(jnp.logical_not(keeps_masks))
    def _():
        remote(own_mask.at[half], mslots1.at[half, me], mone_sem, collector(0)).start()

    copies[2].wait()
    root = [order_ref[i] for i in range(2)]
    root_plane = [(r // 16) * 2 + r % 2 for r in root]
    root_z = [(r // 2) % DEPTH for r in root]
    others = [(q // COLUMNS, collector(q)) for q in mates]
    others = others + [(section, device(section, plane, z)) for section, plane in rest]

    @pl.when(collects)
    def _():
        slots1[half, me] = own[half, :, lanes(slot)]
        wait(source.at[:, :, pl.ds(0, 31 * PIECE // 2)], one_sem.at[1])
        for i in range(2):
            for h in range(2):
                cand[i, h] = slots1[h, root_plane[i]]
        for depth in range(DEPTH):

            @pl.when(z != depth)
            def _(depth=depth):
                remote(cand, slots2.at[z], two_sem, device(half, me, depth)).start()

        slots2[z] = cand[...]

    @pl.when(keeps_masks)
    def _():
        mslots1[0, 0] = own_mask[0]
        wait(source.at[0, :, pl.ds(0, 31 * 128)], mone_sem.at[1])
        for i in range(2):
            for h in range(2):
                mcand[i, h] = mslots1[h, root_plane[i]]
        for depth in column:
            remote(mcand, mslots2.at[z], mtwo_sem, device(half, me, depth)).start()
        mslots2[z] = mcand[...]

    for copy in pair:
        copy.wait()
    for i in range(3, 7):
        copies[i].wait()
    weights = (fir_ref, box_ref, dft_ref, near_ref)
    masks = [own_mask[i].astype(f32) for i in range(2)]
    columns = [m[:, g : g + 1] for m in masks for g in range(SEG)]
    station[0], station[1] = whiten(hour(own), columns, *[w[...] for w in weights])

    @pl.when(collects)
    def _():
        wait(slots2.at[pl.ds(0, DEPTH - 1)], two_sem.at[1])
        for i in range(2):
            picked[i] = slots2[root_z[i], i]
        for section, to in others:
            remote(picked.at[section], source.at[:, :, lanes(slot)], three_sem, to).start()
        source[:, :, lanes(slot)] = picked[half]

    @pl.when(keeps_masks)
    def _():
        wait(mslots2.at[pl.ds(0, DEPTH - 1)], mtwo_sem.at[1])
        for i in range(2):
            mpicked[i] = mslots2[root_z[i], i]
        for section, to in others:
            remote(mpicked.at[section], source_mask, mthree_sem, to).start()
        source_mask[...] = mpicked[0]

    copies[7].wait()

    @pl.when(collects)
    def _():
        wait(source.at[:, :, pl.ds(0, 15 * PIECE)], three_sem.at[1])

    @pl.when(late)
    def _():
        wait(source, three_sem.at[1])

    @pl.when(jnp.logical_not(keeps_masks))
    def _():
        wait(source_mask, mthree_sem.at[1])

    theirs = [source_mask[i].astype(f32) for i in range(2)]
    columns = [m[:, g : g + 1] for m in theirs for g in range(SEG)]
    source_re, source_im = whiten(hour(source), columns, *[w[...] for w in weights])
    for k in range(KT):
        part = slice(128 * k, 128 * (k + 1))
        real = [jnp.zeros((ST, 128), f32)] * ST
        imag = [jnp.zeros((ST, 128), f32)] * ST
        for g in range(SEGS):
            re_s = station[0, ST * g : ST * (g + 1), part]
            im_s = station[1, ST * g : ST * (g + 1), part]
            for n in range(ST):
                re_n = source_re[ST * g + n : ST * g + n + 1, part]
                im_n = source_im[ST * g + n : ST * g + n + 1, part]
                real[n] = real[n] + (re_s * re_n + im_s * im_n)
                imag[n] = imag[n] + (im_s * re_n - re_s * im_n)
        for n in range(ST):
            stack[ST * n : ST * (n + 1), 128 * k : 128 * (k + 1)] = real[n]
            stack[ST * n : ST * (n + 1), NF + 128 * k : NF + 128 * (k + 1)] = imag[n]
    high, low = halves(stack[...])
    first = dot(high, lag_ref[...])
    lagged = first[:, :LAGS] + first[:, LAGS:] + dot(low, lag_ref[:, :LAGS])
    for n in range(ST):
        count = masks[0] * theirs[0][n : n + 1] + masks[1] * theirs[1][n : n + 1]
        count = jnp.maximum(jnp.sum(count, axis=1, keepdims=True), 1.0)
        out_ref[n] = lagged[ST * n : ST * (n + 1)] / count

    @pl.when(collects)
    def _():
        wait(source.at[0, :, pl.ds(0, 15 * PIECE)], one_sem.at[0])
        wait(slots2.at[pl.ds(0, DEPTH - 1)], two_sem.at[0])
        wait(bulk.at[pl.ds(0, 31)], three_sem.at[0])

    @pl.when(late)
    def _():
        wait(source.at[0], one_sem.at[0])

    @pl.when(keeps_masks)
    def _():
        wait(mslots2.at[pl.ds(0, DEPTH - 1)], mtwo_sem.at[0])
        wait(source.at[:, :, pl.ds(0, 31 * 128)], mthree_sem.at[0])

    @pl.when(jnp.logical_not(keeps_masks))
    def _():
        wait(own_mask.at[0], mone_sem.at[0])


def shards(raw_traces, valid_mask, block_order):
    constants = [jnp.asarray(t) for t in tables()]
    hbm = pl.BlockSpec(memory_space=pl.ANY)
    wide = (ST, PIECE)
    flag = (ST, 128)
    pair = pltpu.SemaphoreType.DMA((2,))
    return pl.pallas_call(
        kernel,
        out_shape=jax.ShapeDtypeStruct((ST, ST, LAGS), f32),
        in_specs=[hbm] * (3 + len(constants)),
        out_specs=pl.BlockSpec(memory_space=pltpu.VMEM),
        scratch_shapes=[
            pltpu.VMEM((SEG, ST), jnp.int32),
            pltpu.SMEM(block_order.shape, jnp.int32),
        ]
        + [pltpu.VMEM(c.shape, c.dtype) for c in constants]
        + [
            pltpu.VMEM((2, ST, HALF), bf16),
            pltpu.VMEM((2,) + flag, bf16),
            pltpu.VMEM((2, PLANE) + wide, bf16),
            pltpu.VMEM((2, 2) + wide, bf16),
            pltpu.VMEM((DEPTH, 2, 2) + wide, bf16),
            pltpu.VMEM((2, 2) + wide, bf16),
            pltpu.VMEM((2, ST, HALF), bf16),
            pltpu.VMEM((2 * PLANE, 2) + wide, bf16),
            pltpu.VMEM((2, PLANE) + flag, bf16),
            pltpu.VMEM((2, 2) + flag, bf16),
            pltpu.VMEM((DEPTH, 2, 2) + flag, bf16),
            pltpu.VMEM((2, 2) + flag, bf16),
            pltpu.VMEM((2,) + flag, bf16),
            pltpu.VMEM((2, SEGS * ST, NF), f32),
            pltpu.VMEM((ST * ST, 2 * NF), f32),
            pltpu.SemaphoreType.DMA((3 + len(constants),)),
            pair, pair, pair, pair, pair, pair, pair, pair,
        ],
        compiler_params=pltpu.CompilerParams(
            collective_id=0, has_side_effects=True, vmem_limit_bytes=VMEM_KIB << 10
        ),
    )(
        *[
            pltpu.with_memory_space_constraint(a, pltpu.HBM)
            for a in (raw_traces, valid_mask.T, block_order, *constants)
        ]
    )


def solution(mesh):
    return jax.shard_map(
        shards,
        mesh=mesh,
        in_specs=(P("blk", "section"), P("blk", "section"), P()),
        out_specs=P("section", "blk", None),
        check_vma=False,
    )
```

```python
import math

import jax
import jax.numpy as jnp
import ml_dtypes
import numpy as np
from jax import lax
from jax.experimental import pallas as pl
from jax.experimental.pallas import tpu as pltpu
from jax.sharding import PartitionSpec as P

L = 1024
NF = 384
BIN_LO = 8
LAGS = 256
TAPS = 33
HW = 50
WF = 32
KT = NF // 128
SEGS = 8
SEG = 4
HALF = SEG * L
ST = 8
PIECE = 256
VMEM_KIB = 32768
PLANE = 16
DEPTH = 8
N_BLK = 128
MESH = pl.DeviceIdType.MESH
CHIPS = [(x, 0) for x in range(4)] + [(0, y) for y in range(1, 4)] + [(1, 1)]
REST = [(x, y) for y in range(4) for x in range(4) if (x, y) not in CHIPS]
f32 = jnp.float32
bf16 = jnp.bfloat16


def split(values):
    high = values.astype(np.float32).astype(ml_dtypes.bfloat16)
    low = (values - high.astype(np.float64)).astype(ml_dtypes.bfloat16)
    return high, low


def tables():
    half = (TAPS - 1) // 2
    k = np.arange(-half, half + 1).astype(np.float64)
    a, b = BIN_LO / L, (BIN_LO + NF) / L
    taps = (0.5 + 0.5 * np.cos(2 * np.pi * k / (TAPS + 1))) * (
        2 * b * np.sinc(2 * b * k) - 2 * a * np.sinc(2 * a * k)
    )
    shift = np.arange(128)[None, :] + 128 - np.arange(384)[:, None]
    band = np.where(np.abs(shift) <= half, taps[np.clip(shift + half, 0, TAPS - 1)], 0.0)
    fir = np.concatenate(split(band), axis=1)
    box = (np.abs(shift) <= HW).astype(ml_dtypes.bfloat16)
    box = np.concatenate([box, box], axis=0)
    bins = BIN_LO + np.arange(NF)
    phase = (np.arange(L)[:, None] * bins[None, :]) % L * (2 * np.pi / L)
    dft = np.concatenate([np.cos(phase), -np.sin(phase)], axis=1)
    dft = dft.astype(np.float32).astype(ml_dtypes.bfloat16)
    near = np.abs(np.arange(NF)[:, None] - np.arange(NF)[None, :]) <= WF
    near = near.astype(ml_dtypes.bfloat16)
    phase = (bins[:, None] * (np.arange(LAGS) - LAGS // 2)[None, :]) % L * (2 * np.pi / L)
    lag = np.concatenate([np.cos(phase), -np.sin(phase)], axis=0) / math.sqrt(NF)
    lag = np.concatenate(split(lag), axis=1)
    return fir, box, dft, near, lag


def dot(a, b):
    return jnp.dot(a, b, preferred_element_type=f32)


def halves(x):
    high = x.astype(bf16)
    return high, (x - high.astype(f32)).astype(bf16)


def whiten(tiles, masks, fir, box, dft, near):
    count = len(tiles)
    zero = jnp.zeros((ST, 128), f32)
    left = jnp.concatenate([zero, zero] + tiles, axis=0).astype(bf16)
    mid = jnp.concatenate([zero] + tiles + [zero], axis=0).astype(bf16)
    right = jnp.concatenate(tiles + [zero, zero], axis=0).astype(bf16)
    both = dot(jnp.concatenate([left, mid, right], axis=1), fir)
    filtered = both[:, :128] + both[:, 128:]
    size = jnp.abs(filtered)
    rows = count * ST
    parts = [halves(size[ST * i : ST * i + rows]) for i in range(3)]
    window = dot(jnp.concatenate([p[0] for p in parts] + [p[1] for p in parts], axis=1), box)
    normalized = filtered[ST : ST + rows] / (window * (1.0 / (2 * HW + 1)) + 1e-06)
    per = L // 128
    lanes = [
        jnp.concatenate(
            [normalized[(g * per + t) * ST : (g * per + t + 1) * ST] for g in range(SEGS)], axis=0
        )
        for t in range(per)
    ]
    spectra = dot(jnp.concatenate(lanes, axis=1).astype(bf16), dft)
    re, im = spectra[:, :NF], spectra[:, NF:]
    high, low = halves(jnp.sqrt(re * re + im * im))
    smooth = dot(high, near) + dot(low, near)
    factor = jnp.concatenate(masks, axis=0) / (smooth * (1.0 / (2 * WF + 1)) + 1e-06)
    return (re * factor).astype(bf16).astype(f32), (im * factor).astype(bf16).astype(f32)


def hour(ref):
    return [ref[h, :, 128 * i : 128 * (i + 1)].astype(f32) for h in range(2) for i in range(HALF // 128)]


def kernel(
    raw_hbm, mask_hbm, order_hbm, fir_hbm, box_hbm, dft_hbm, near_hbm, lag_hbm, out_ref,
    mask_ref, order_ref, fir_ref, box_ref, dft_ref, near_ref, lag_ref,
    own, own_mask, slots1, cand, slots2, picked, source, bulk,
    mslots1, mcand, mslots2, mpicked, source_mask, station, stack,
    copy_sem, pair_sem, mpair_sem, one_sem, two_sem, three_sem, mone_sem, mtwo_sem, mthree_sem,
):
    half = lax.axis_index("section")
    blk = lax.axis_index("blk")
    me = (blk // 16) * 2 + blk % 2
    x = (blk // 64) * 2 + half
    y = (blk // 16) % 4
    z = (blk // 2) % DEPTH
    core = blk % 2
    collects = x * y < 2
    late = x * y >= 2
    chip = x + y + 3 * ((y + 3) // 4) + 2 * x * y
    slot = jnp.where(collects, chip * 2 + core, PLANE)
    keeps_masks = half * N_BLK + blk == z * 2

    def device(chip, core):
        return (chip[0] % 2, (chip[0] // 2) * 64 + chip[1] * 16 + core + z * 2)

    collectors = [device(chip, i) for chip in CHIPS for i in range(2)]
    rest = [device(chip, i) for chip in REST for i in range(2)]

    def remote(src, dst, sems, to):
        return pltpu.make_async_remote_copy(
            src_ref=src, dst_ref=dst, send_sem=sems.at[0], recv_sem=sems.at[1],
            device_id=to, device_id_type=MESH,
        )

    def wait(ref, sem):
        pltpu.make_async_copy(ref, ref, sem).wait()

    def lanes(q):
        return pl.ds(q * PIECE if isinstance(q, int) else pl.multiple_of(q * PIECE, PIECE), PIECE)

    def above(depth):
        return (half, blk + (depth - z) * 2)

    other = (1 - half, blk)
    barrier = pltpu.get_barrier_semaphore()

    def signal(to):
        pl.semaphore_signal(barrier, inc=1, device_id=to, device_id_type=MESH)

    @pl.when(collects)
    def _():
        for depth in range(DEPTH):

            @pl.when(z != depth)
            def _(depth=depth):
                signal(above(depth))

        for q, to in enumerate(collectors):

            @pl.when(slot != q)
            def _(to=to):
                signal(to)

        for to in rest:
            signal(to)

    @pl.when(late)
    def _():
        signal(other)

    mine = own.at[half]
    copies = [
        pltpu.make_async_copy(src, dst, copy_sem.at[i])
        for i, (src, dst) in enumerate(
            (
                (raw_hbm, mine), (mask_hbm, mask_ref), (order_hbm, order_ref),
                (fir_hbm, fir_ref), (box_hbm, box_ref), (dft_hbm, dft_ref),
                (near_hbm, near_ref), (lag_hbm, lag_ref),
            )
        )
    ]
    for copy in copies:
        copy.start()
    copies[1].wait()
    flags = mask_ref[...].astype(f32)
    eye = lax.broadcasted_iota(jnp.int32, (ST, ST), 0) == lax.broadcasted_iota(
        jnp.int32, (ST, ST), 1
    )
    lane = lax.broadcasted_iota(jnp.int32, (ST, 128), 1)
    tile = jnp.zeros((ST, 128), f32)
    for g in range(SEG):
        row = jnp.where(eye, jnp.broadcast_to(flags[g : g + 1], (ST, ST)), 0.0)
        tile = jnp.where(lane == g, jnp.sum(row, axis=1, keepdims=True), tile)
    own_mask[half] = tile.astype(bf16)
    copies[0].wait()

    @pl.when(collects & (y < 2))
    def _():
        pl.semaphore_wait(barrier, DEPTH - 1 + PLANE - 1)

    @pl.when(collects & (y >= 2))
    def _():
        pl.semaphore_wait(barrier, DEPTH - 1 + PLANE)

    @pl.when(late & (x < 2))
    def _():
        pl.semaphore_wait(barrier, PLANE)

    @pl.when(late & (x >= 2))
    def _():
        pl.semaphore_wait(barrier, PLANE + 1)

    for q, to in enumerate(collectors):

        @pl.when(slot != q)
        def _(q=q, to=to):
            remote(own.at[half, :, lanes(q)], slots1.at[half, me], one_sem, to).start()

    pair = [
        remote(mine, mine, pair_sem, other),
        remote(own_mask.at[half], own_mask.at[half], mpair_sem, other),
    ]
    for copy in pair:
        copy.start()

    @pl.when(jnp.logical_not(keeps_masks))
    def _():
        remote(own_mask.at[half], mslots1.at[half, me], mone_sem, collectors[0]).start()

    copies[2].wait()
    root = [order_ref[i] for i in range(2)]
    root_plane = [(r // 16) * 2 + r % 2 for r in root]
    root_z = [(r // 2) % DEPTH for r in root]

    @pl.when(collects)
    def _():
        slots1[half, me] = own[half, :, lanes(slot)]
        wait(source.at[:, :, pl.ds(0, 31 * PIECE // 2)], one_sem.at[1])
        for i in range(2):
            for h in range(2):
                cand[i, h] = slots1[h, root_plane[i]]
        for depth in range(DEPTH):

            @pl.when(z != depth)
            def _(depth=depth):
                remote(cand, slots2.at[z], two_sem, above(depth)).start()

        slots2[z] = cand[...]

    @pl.when(keeps_masks)
    def _():
        mslots1[0, 0] = own_mask[0]
        wait(source.at[0, :, pl.ds(0, 31 * 128)], mone_sem.at[1])
        for i in range(2):
            for h in range(2):
                mcand[i, h] = mslots1[h, root_plane[i]]
        for depth in range(DEPTH):

            @pl.when(z != depth)
            def _(depth=depth):
                remote(mcand, mslots2.at[z], mtwo_sem, above(depth)).start()

        mslots2[z] = mcand[...]

    for copy in pair:
        copy.wait()
    for i in range(3, 7):
        copies[i].wait()
    weights = (fir_ref, box_ref, dft_ref, near_ref)
    masks = [own_mask[i].astype(f32) for i in range(2)]
    columns = [m[:, g : g + 1] for m in masks for g in range(SEG)]
    station[0], station[1] = whiten(hour(own), columns, *[w[...] for w in weights])

    @pl.when(collects)
    def _():
        wait(slots2.at[pl.ds(0, DEPTH - 1)], two_sem.at[1])
        for i in range(2):
            picked[i] = slots2[root_z[i], i]
        for q, to in enumerate(collectors):

            @pl.when(slot != q)
            def _(to=to):
                remote(picked.at[to[0]], source.at[:, :, lanes(slot)], three_sem, to).start()

        for to in rest:
            remote(picked.at[to[0]], source.at[:, :, lanes(slot)], three_sem, to).start()
        source[:, :, lanes(slot)] = picked[half]

    @pl.when(keeps_masks)
    def _():
        wait(mslots2.at[pl.ds(0, DEPTH - 1)], mtwo_sem.at[1])
        for i in range(2):
            mpicked[i] = mslots2[root_z[i], i]
        for to in collectors[1:] + rest:
            remote(mpicked.at[to[0]], source_mask, mthree_sem, to).start()
        source_mask[...] = mpicked[0]

    copies[7].wait()

    @pl.when(collects)
    def _():
        wait(source.at[:, :, pl.ds(0, 15 * PIECE)], three_sem.at[1])

    @pl.when(late)
    def _():
        wait(source, three_sem.at[1])

    @pl.when(jnp.logical_not(keeps_masks))
    def _():
        wait(source_mask, mthree_sem.at[1])

    theirs = [source_mask[i].astype(f32) for i in range(2)]
    columns = [m[:, g : g + 1] for m in theirs for g in range(SEG)]
    source_re, source_im = whiten(hour(source), columns, *[w[...] for w in weights])
    for k in range(KT):
        part = slice(128 * k, 128 * (k + 1))
        real = [jnp.zeros((ST, 128), f32)] * ST
        imag = [jnp.zeros((ST, 128), f32)] * ST
        for g in range(SEGS):
            re_s = station[0, ST * g : ST * (g + 1), part]
            im_s = station[1, ST * g : ST * (g + 1), part]
            for n in range(ST):
                re_n = source_re[ST * g + n : ST * g + n + 1, part]
                im_n = source_im[ST * g + n : ST * g + n + 1, part]
                real[n] = real[n] + (re_s * re_n + im_s * im_n)
                imag[n] = imag[n] + (im_s * re_n - re_s * im_n)
        for n in range(ST):
            stack[ST * n : ST * (n + 1), 128 * k : 128 * (k + 1)] = real[n]
            stack[ST * n : ST * (n + 1), NF + 128 * k : NF + 128 * (k + 1)] = imag[n]
    high, low = halves(stack[...])
    first = dot(high, lag_ref[...])
    lagged = first[:, :LAGS] + first[:, LAGS:] + dot(low, lag_ref[:, :LAGS])
    for n in range(ST):
        count = masks[0] * theirs[0][n : n + 1] + masks[1] * theirs[1][n : n + 1]
        count = jnp.maximum(jnp.sum(count, axis=1, keepdims=True), 1.0)
        out_ref[n] = lagged[ST * n : ST * (n + 1)] / count

    @pl.when(collects)
    def _():
        wait(source.at[0, :, pl.ds(0, 15 * PIECE)], one_sem.at[0])
        wait(slots2.at[pl.ds(0, DEPTH - 1)], two_sem.at[0])
        wait(bulk.at[pl.ds(0, 31)], three_sem.at[0])

    @pl.when(late)
    def _():
        wait(source.at[0], one_sem.at[0])

    @pl.when(keeps_masks)
    def _():
        wait(mslots2.at[pl.ds(0, DEPTH - 1)], mtwo_sem.at[0])
        wait(source.at[:, :, pl.ds(0, 31 * 128)], mthree_sem.at[0])

    @pl.when(jnp.logical_not(keeps_masks))
    def _():
        wait(own_mask.at[0], mone_sem.at[0])


def shards(raw_traces, valid_mask, block_order):
    constants = [jnp.asarray(t) for t in tables()]
    hbm = pl.BlockSpec(memory_space=pl.ANY)
    wide = (ST, PIECE)
    flag = (ST, 128)
    pair = pltpu.SemaphoreType.DMA((2,))
    return pl.pallas_call(
        kernel,
        out_shape=jax.ShapeDtypeStruct((ST, ST, LAGS), f32),
        in_specs=[hbm] * (3 + len(constants)),
        out_specs=pl.BlockSpec(memory_space=pltpu.VMEM),
        scratch_shapes=[
            pltpu.VMEM((SEG, ST), jnp.int32),
            pltpu.SMEM(block_order.shape, jnp.int32),
        ]
        + [pltpu.VMEM(c.shape, c.dtype) for c in constants]
        + [
            pltpu.VMEM((2, ST, HALF), bf16),
            pltpu.VMEM((2,) + flag, bf16),
            pltpu.VMEM((2, PLANE) + wide, bf16),
            pltpu.VMEM((2, 2) + wide, bf16),
            pltpu.VMEM((DEPTH, 2, 2) + wide, bf16),
            pltpu.VMEM((2, 2) + wide, bf16),
            pltpu.VMEM((2, ST, HALF), bf16),
            pltpu.VMEM((2 * PLANE, 2) + wide, bf16),
            pltpu.VMEM((2, PLANE) + flag, bf16),
            pltpu.VMEM((2, 2) + flag, bf16),
            pltpu.VMEM((DEPTH, 2, 2) + flag, bf16),
            pltpu.VMEM((2, 2) + flag, bf16),
            pltpu.VMEM((2,) + flag, bf16),
            pltpu.VMEM((2, SEGS * ST, NF), f32),
            pltpu.VMEM((ST * ST, 2 * NF), f32),
            pltpu.SemaphoreType.DMA((3 + len(constants),)),
            pair, pair, pair, pair, pair, pair, pair, pair,
        ],
        compiler_params=pltpu.CompilerParams(
            collective_id=0, has_side_effects=True, vmem_limit_bytes=VMEM_KIB << 10
        ),
    )(
        *[
            pltpu.with_memory_space_constraint(a, pltpu.HBM)
            for a in (raw_traces, valid_mask.T, block_order, *constants)
        ]
    )


def solution(mesh):
    return jax.shard_map(
        shards,
        mesh=mesh,
        in_specs=(P("blk", "section"), P("blk", "section"), P()),
        out_specs=P("section", "blk", None),
        check_vma=False,
    )
```

```python
import math

import jax
import jax.numpy as jnp
import ml_dtypes
import numpy as np
from jax import lax
from jax.experimental import pallas as pl
from jax.experimental.pallas import tpu as pltpu
from jax.sharding import PartitionSpec as P

L = 1024
NF = 384
BIN_LO = 8
LAGS = 256
TAPS = 33
HW = 50
WF = 32
KT = NF // 128
SEGS = 8
SEG = 4
HALF = SEG * L
ST = 8
PIECE = 256
VMEM_KIB = 32768
PLANE = 16
DEPTH = 8
N_BLK = 128
MESH = pl.DeviceIdType.MESH
CHIPS = [(x, 0) for x in range(4)] + [(0, y) for y in range(1, 4)] + [(1, 1)]
REST = [(x, y) for y in range(4) for x in range(4) if (x, y) not in CHIPS]
f32 = jnp.float32
bf16 = jnp.bfloat16


def split(values):
    high = values.astype(np.float32).astype(ml_dtypes.bfloat16)
    low = (values - high.astype(np.float64)).astype(ml_dtypes.bfloat16)
    return high, low


def tables():
    half = (TAPS - 1) // 2
    k = np.arange(-half, half + 1).astype(np.float64)
    a, b = BIN_LO / L, (BIN_LO + NF) / L
    taps = (0.5 + 0.5 * np.cos(2 * np.pi * k / (TAPS + 1))) * (
        2 * b * np.sinc(2 * b * k) - 2 * a * np.sinc(2 * a * k)
    )
    shift = np.arange(128)[None, :] + 128 - np.arange(384)[:, None]
    band = np.where(np.abs(shift) <= half, taps[np.clip(shift + half, 0, TAPS - 1)], 0.0)
    fir = np.concatenate(split(band), axis=1)
    box = (np.abs(shift) <= HW).astype(ml_dtypes.bfloat16)
    bins = BIN_LO + np.arange(NF)
    phase = (np.arange(L)[:, None] * bins[None, :]) % L * (2 * np.pi / L)
    dft = np.concatenate([np.cos(phase), -np.sin(phase)], axis=1)
    dft = dft.astype(np.float32).astype(ml_dtypes.bfloat16)
    near = np.abs(np.arange(NF)[:, None] - np.arange(NF)[None, :]) <= WF
    near = near.astype(ml_dtypes.bfloat16)
    phase = (bins[:, None] * (np.arange(LAGS) - LAGS // 2)[None, :]) % L * (2 * np.pi / L)
    lag = np.concatenate([np.cos(phase), -np.sin(phase)], axis=0) / math.sqrt(NF)
    lag = np.concatenate(split(lag), axis=1)
    return fir, box, dft, near, lag


def dot(a, b):
    return jnp.dot(a, b, preferred_element_type=f32)


def halves(x):
    high = x.astype(bf16)
    return high, (x - high.astype(f32)).astype(bf16)


def whiten(tiles, masks, fir, box, dft, near):
    zero = jnp.zeros((ST, 128), f32)
    rows = len(tiles) * ST
    edge = rows + 2 * ST
    padded = [zero, zero] + tiles + [zero, zero]
    wide = jnp.concatenate(padded, axis=0).astype(bf16)
    mid = jnp.concatenate(padded[1:-1], axis=0).astype(bf16)
    both = dot(jnp.concatenate([wide[:edge], mid, wide[2 * ST :]], axis=1), fir)
    filtered = both[:, :128] + both[:, 128:]
    size = jnp.abs(filtered)
    wide = size.astype(bf16)
    mid = size[ST : ST + rows].astype(bf16)
    window = dot(jnp.concatenate([wide[:rows], mid, wide[2 * ST :]], axis=1), box)
    normalized = filtered[ST : ST + rows] / (window * (1.0 / (2 * HW + 1)) + 1e-06)
    per = L // 128
    lanes = [
        jnp.concatenate(
            [normalized[(g * per + t) * ST : (g * per + t + 1) * ST] for g in range(SEGS)], axis=0
        )
        for t in range(per)
    ]
    spectra = dot(jnp.concatenate(lanes, axis=1).astype(bf16), dft)
    re, im = spectra[:, :NF], spectra[:, NF:]
    smooth = dot(jnp.sqrt(re * re + im * im).astype(bf16), near)
    factor = jnp.concatenate(masks, axis=0) / (smooth * (1.0 / (2 * WF + 1)) + 1e-06)
    return (re * factor).astype(bf16).astype(f32), (im * factor).astype(bf16).astype(f32)


def hour(ref):
    return [ref[h, :, 128 * i : 128 * (i + 1)].astype(f32) for h in range(2) for i in range(HALF // 128)]


def kernel(
    raw_hbm, mask_hbm, order_hbm, fir_hbm, box_hbm, dft_hbm, near_hbm, lag_hbm, out_ref,
    mask_ref, order_ref, fir_ref, box_ref, dft_ref, near_ref, lag_ref,
    own, own_mask, slots1, cand, slots2, picked, source, bulk,
    mslots1, mcand, mslots2, mpicked, source_mask, station, stack,
    copy_sem, pair_sem, mpair_sem, one_sem, two_sem, three_sem, mone_sem, mtwo_sem, mthree_sem,
):
    half = lax.axis_index("section")
    blk = lax.axis_index("blk")
    me = (blk // 16) * 2 + blk % 2
    x = (blk // 64) * 2 + half
    y = (blk // 16) % 4
    z = (blk // 2) % DEPTH
    core = blk % 2
    collects = x * y < 2
    late = x * y >= 2
    chip = x + y + 3 * ((y + 3) // 4) + 2 * x * y
    slot = jnp.where(collects, chip * 2 + core, PLANE)
    keeps_masks = half * N_BLK + blk == z * 2

    def device(chip, core):
        return (chip[0] % 2, (chip[0] // 2) * 64 + chip[1] * 16 + core + z * 2)

    collectors = [device(chip, i) for chip in CHIPS for i in range(2)]
    rest = [device(chip, i) for chip in REST for i in range(2)]

    def remote(src, dst, sems, to):
        return pltpu.make_async_remote_copy(
            src_ref=src, dst_ref=dst, send_sem=sems.at[0], recv_sem=sems.at[1],
            device_id=to, device_id_type=MESH,
        )

    def wait(ref, sem):
        pltpu.make_async_copy(ref, ref, sem).wait()

    def lanes(q):
        return pl.ds(q * PIECE if isinstance(q, int) else pl.multiple_of(q * PIECE, PIECE), PIECE)

    def above(depth):
        return (half, blk + (depth - z) * 2)

    other = (1 - half, blk)
    barrier = pltpu.get_barrier_semaphore()

    def signal(to):
        pl.semaphore_signal(barrier, inc=1, device_id=to, device_id_type=MESH)

    @pl.when(collects)
    def _():
        for to in rest:
            signal(to)

        for q, to in enumerate(collectors):

            @pl.when(slot != q)
            def _(to=to):
                signal(to)

        for depth in range(DEPTH):

            @pl.when(z != depth)
            def _(depth=depth):
                signal(above(depth))

    @pl.when(late)
    def _():
        signal(other)

    mine = own.at[half]
    copies = [
        pltpu.make_async_copy(src, dst, copy_sem.at[i])
        for i, (src, dst) in enumerate(
            (
                (raw_hbm, mine), (mask_hbm, mask_ref), (order_hbm, order_ref),
                (fir_hbm, fir_ref), (box_hbm, box_ref), (dft_hbm, dft_ref),
                (near_hbm, near_ref), (lag_hbm, lag_ref),
            )
        )
    ]
    for copy in copies:
        copy.start()
    copies[1].wait()
    flags = mask_ref[...].astype(f32)
    eye = lax.broadcasted_iota(jnp.int32, (ST, ST), 0) == lax.broadcasted_iota(
        jnp.int32, (ST, ST), 1
    )
    lane = lax.broadcasted_iota(jnp.int32, (ST, 128), 1)
    tile = jnp.zeros((ST, 128), f32)
    for g in range(SEG):
        row = jnp.where(eye, jnp.broadcast_to(flags[g : g + 1], (ST, ST)), 0.0)
        tile = jnp.where(lane == g, jnp.sum(row, axis=1, keepdims=True), tile)
    own_mask[half] = tile.astype(bf16)
    copies[0].wait()

    @pl.when(collects & (y < 2))
    def _():
        pl.semaphore_wait(barrier, DEPTH - 1 + PLANE - 1)

    @pl.when(collects & (y >= 2))
    def _():
        pl.semaphore_wait(barrier, DEPTH - 1 + PLANE)

    @pl.when(late & (x < 2))
    def _():
        pl.semaphore_wait(barrier, PLANE)

    @pl.when(late & (x >= 2))
    def _():
        pl.semaphore_wait(barrier, PLANE + 1)

    for q, to in enumerate(collectors):

        @pl.when(slot != q)
        def _(q=q, to=to):
            remote(own.at[half, :, lanes(q)], slots1.at[half, me], one_sem, to).start()

    pair = [
        remote(mine, mine, pair_sem, other),
        remote(own_mask.at[half], own_mask.at[half], mpair_sem, other),
    ]
    for copy in pair:
        copy.start()

    @pl.when(jnp.logical_not(keeps_masks))
    def _():
        remote(own_mask.at[half], mslots1.at[half, me], mone_sem, collectors[0]).start()

    copies[2].wait()
    root = [order_ref[i] for i in range(2)]
    root_plane = [(r // 16) * 2 + r % 2 for r in root]
    root_z = [(r // 2) % DEPTH for r in root]

    @pl.when(collects)
    def _():
        slots1[half, me] = own[half, :, lanes(slot)]
        wait(source.at[:, :, pl.ds(0, 31 * PIECE // 2)], one_sem.at[1])
        for i in range(2):
            for h in range(2):
                cand[i, h] = slots1[h, root_plane[i]]
        for depth in range(DEPTH):

            @pl.when(z != depth)
            def _(depth=depth):
                remote(cand, slots2.at[z], two_sem, above(depth)).start()

        slots2[z] = cand[...]

    @pl.when(keeps_masks)
    def _():
        mslots1[0, 0] = own_mask[0]
        wait(source.at[0, :, pl.ds(0, 31 * 128)], mone_sem.at[1])
        for i in range(2):
            for h in range(2):
                mcand[i, h] = mslots1[h, root_plane[i]]
        for depth in range(DEPTH):

            @pl.when(z != depth)
            def _(depth=depth):
                remote(mcand, mslots2.at[z], mtwo_sem, above(depth)).start()

        mslots2[z] = mcand[...]

    for copy in pair:
        copy.wait()
    for i in range(3, 7):
        copies[i].wait()
    weights = (fir_ref, box_ref, dft_ref, near_ref)
    masks = [own_mask[i].astype(f32) for i in range(2)]
    columns = [m[:, g : g + 1] for m in masks for g in range(SEG)]
    station[0], station[1] = whiten(hour(own), columns, *[w[...] for w in weights])

    @pl.when(collects)
    def _():
        wait(slots2.at[pl.ds(0, DEPTH - 1)], two_sem.at[1])
        for i in range(2):
            picked[i] = slots2[root_z[i], i]
        for q, to in enumerate(collectors):

            @pl.when(slot != q)
            def _(to=to):
                remote(picked.at[to[0]], source.at[:, :, lanes(slot)], three_sem, to).start()

        for to in rest:
            remote(picked.at[to[0]], source.at[:, :, lanes(slot)], three_sem, to).start()
        source[:, :, lanes(slot)] = picked[half]

    @pl.when(keeps_masks)
    def _():
        wait(mslots2.at[pl.ds(0, DEPTH - 1)], mtwo_sem.at[1])
        for i in range(2):
            mpicked[i] = mslots2[root_z[i], i]
        for to in collectors[1:] + rest:
            remote(mpicked.at[to[0]], source_mask, mthree_sem, to).start()
        source_mask[...] = mpicked[0]

    copies[7].wait()

    @pl.when(collects)
    def _():
        wait(source.at[:, :, pl.ds(0, 15 * PIECE)], three_sem.at[1])

    @pl.when(late)
    def _():
        wait(source, three_sem.at[1])

    @pl.when(jnp.logical_not(keeps_masks))
    def _():
        wait(source_mask, mthree_sem.at[1])

    theirs = [source_mask[i].astype(f32) for i in range(2)]
    columns = [m[:, g : g + 1] for m in theirs for g in range(SEG)]
    source_re, source_im = whiten(hour(source), columns, *[w[...] for w in weights])
    for k in range(KT):
        part = slice(128 * k, 128 * (k + 1))
        real = [jnp.zeros((ST, 128), f32)] * ST
        imag = [jnp.zeros((ST, 128), f32)] * ST
        for g in range(SEGS):
            re_s = station[0, ST * g : ST * (g + 1), part]
            im_s = station[1, ST * g : ST * (g + 1), part]
            for n in range(ST):
                re_n = source_re[ST * g + n : ST * g + n + 1, part]
                im_n = source_im[ST * g + n : ST * g + n + 1, part]
                real[n] = real[n] + (re_s * re_n + im_s * im_n)
                imag[n] = imag[n] + (im_s * re_n - re_s * im_n)
        for n in range(ST):
            stack[ST * n : ST * (n + 1), 128 * k : 128 * (k + 1)] = real[n]
            stack[ST * n : ST * (n + 1), NF + 128 * k : NF + 128 * (k + 1)] = imag[n]
    high, low = halves(stack[...])
    first = dot(high, lag_ref[...])
    lagged = first[:, :LAGS] + first[:, LAGS:] + dot(low, lag_ref[:, :LAGS])
    for n in range(ST):
        count = masks[0] * theirs[0][n : n + 1] + masks[1] * theirs[1][n : n + 1]
        count = jnp.maximum(jnp.sum(count, axis=1, keepdims=True), 1.0)
        out_ref[n] = lagged[ST * n : ST * (n + 1)] / count

    @pl.when(collects)
    def _():
        wait(source.at[0, :, pl.ds(0, 15 * PIECE)], one_sem.at[0])
        wait(slots2.at[pl.ds(0, DEPTH - 1)], two_sem.at[0])
        wait(bulk.at[pl.ds(0, 31)], three_sem.at[0])

    @pl.when(late)
    def _():
        wait(source.at[0], one_sem.at[0])

    @pl.when(keeps_masks)
    def _():
        wait(mslots2.at[pl.ds(0, DEPTH - 1)], mtwo_sem.at[0])
        wait(source.at[:, :, pl.ds(0, 31 * 128)], mthree_sem.at[0])

    @pl.when(jnp.logical_not(keeps_masks))
    def _():
        wait(own_mask.at[0], mone_sem.at[0])


def shards(raw_traces, valid_mask, block_order):
    constants = [jnp.asarray(t) for t in tables()]
    hbm = pl.BlockSpec(memory_space=pl.ANY)
    wide = (ST, PIECE)
    flag = (ST, 128)
    pair = pltpu.SemaphoreType.DMA((2,))
    return pl.pallas_call(
        kernel,
        out_shape=jax.ShapeDtypeStruct((ST, ST, LAGS), f32),
        in_specs=[hbm] * (3 + len(constants)),
        out_specs=pl.BlockSpec(memory_space=pltpu.VMEM),
        scratch_shapes=[
            pltpu.VMEM((SEG, ST), jnp.int32),
            pltpu.SMEM(block_order.shape, jnp.int32),
        ]
        + [pltpu.VMEM(c.shape, c.dtype) for c in constants]
        + [
            pltpu.VMEM((2, ST, HALF), bf16),
            pltpu.VMEM((2,) + flag, bf16),
            pltpu.VMEM((2, PLANE) + wide, bf16),
            pltpu.VMEM((2, 2) + wide, bf16),
            pltpu.VMEM((DEPTH, 2, 2) + wide, bf16),
            pltpu.VMEM((2, 2) + wide, bf16),
            pltpu.VMEM((2, ST, HALF), bf16),
            pltpu.VMEM((2 * PLANE, 2) + wide, bf16),
            pltpu.VMEM((2, PLANE) + flag, bf16),
            pltpu.VMEM((2, 2) + flag, bf16),
            pltpu.VMEM((DEPTH, 2, 2) + flag, bf16),
            pltpu.VMEM((2, 2) + flag, bf16),
            pltpu.VMEM((2,) + flag, bf16),
            pltpu.VMEM((2, SEGS * ST, NF), f32),
            pltpu.VMEM((ST * ST, 2 * NF), f32),
            pltpu.SemaphoreType.DMA((3 + len(constants),)),
            pair, pair, pair, pair, pair, pair, pair, pair,
        ],
        compiler_params=pltpu.CompilerParams(
            collective_id=0, has_side_effects=True, vmem_limit_bytes=VMEM_KIB << 10
        ),
    )(
        *[
            pltpu.with_memory_space_constraint(a, pltpu.HBM)
            for a in (raw_traces, valid_mask.T, block_order, *constants)
        ]
    )


def solution(mesh):
    return jax.shard_map(
        shards,
        mesh=mesh,
        in_specs=(P("blk", "section"), P("blk", "section"), P()),
        out_specs=P("section", "blk", None),
        check_vma=False,
    )
```

```python
import math

import jax
import jax.numpy as jnp
import ml_dtypes
import numpy as np
from jax import lax
from jax.experimental import pallas as pl
from jax.experimental.pallas import tpu as pltpu
from jax.sharding import PartitionSpec as P

L = 1024
NF = 384
BIN_LO = 8
LAGS = 256
TAPS = 33
HW = 50
WF = 32
KT = NF // 128
SEGS = 8
SEG = 4
HALF = SEG * L
ST = 8
PIECE = 256
VMEM_KIB = 32768
PLANE = 16
DEPTH = 8
N_BLK = 128
MESH = pl.DeviceIdType.MESH
CHIPS = [(x, 0) for x in range(4)] + [(0, y) for y in range(1, 4)] + [(1, 1)]
REST = [(x, y) for y in range(4) for x in range(4) if (x, y) not in CHIPS]
f32 = jnp.float32
bf16 = jnp.bfloat16


def split(values):
    high = values.astype(np.float32).astype(ml_dtypes.bfloat16)
    low = (values - high.astype(np.float64)).astype(ml_dtypes.bfloat16)
    return high, low


def tables():
    half = (TAPS - 1) // 2
    k = np.arange(-half, half + 1).astype(np.float64)
    a, b = BIN_LO / L, (BIN_LO + NF) / L
    taps = (0.5 + 0.5 * np.cos(2 * np.pi * k / (TAPS + 1))) * (
        2 * b * np.sinc(2 * b * k) - 2 * a * np.sinc(2 * a * k)
    )
    shift = np.arange(128)[None, :] + 128 - np.arange(384)[:, None]
    band = np.where(np.abs(shift) <= half, taps[np.clip(shift + half, 0, TAPS - 1)], 0.0)
    fir = np.concatenate(split(band), axis=1)
    box = (np.abs(shift) <= HW).astype(ml_dtypes.bfloat16)
    bins = BIN_LO + np.arange(NF)
    phase = (np.arange(L)[:, None] * bins[None, :]) % L * (2 * np.pi / L)
    dft = np.concatenate([np.cos(phase), -np.sin(phase)], axis=1)
    dft = dft.astype(np.float32).astype(ml_dtypes.bfloat16)
    near = np.abs(np.arange(NF)[:, None] - np.arange(NF)[None, :]) <= WF
    near = near.astype(ml_dtypes.bfloat16)
    phase = (bins[:, None] * (np.arange(LAGS) - LAGS // 2)[None, :]) % L * (2 * np.pi / L)
    lag = np.concatenate([np.cos(phase), -np.sin(phase)], axis=0) / math.sqrt(NF)
    lag = np.concatenate(split(lag), axis=1)
    return fir, box, dft, near, lag


def dot(a, b):
    return jnp.dot(a, b, preferred_element_type=f32)


def halves(x):
    high = x.astype(bf16)
    return high, (x - high.astype(f32)).astype(bf16)


def whiten(tiles, masks, fir, box, dft, near):
    zero = jnp.zeros((ST, 128), f32)
    rows = len(tiles) * ST
    edge = rows + 2 * ST
    padded = [zero, zero] + tiles + [zero, zero]
    wide = jnp.concatenate(padded, axis=0).astype(bf16)
    mid = jnp.concatenate(padded[1:-1], axis=0).astype(bf16)
    both = dot(jnp.concatenate([wide[:edge], mid, wide[2 * ST :]], axis=1), fir)
    filtered = both[:, :128] + both[:, 128:]
    size = jnp.abs(filtered)
    wide = size.astype(bf16)
    mid = size[ST : ST + rows].astype(bf16)
    window = dot(jnp.concatenate([wide[:rows], mid, wide[2 * ST :]], axis=1), box)
    normalized = filtered[ST : ST + rows] / (window * (1.0 / (2 * HW + 1)) + 1e-06)
    per = L // 128
    lanes = [
        jnp.concatenate(
            [normalized[(g * per + t) * ST : (g * per + t + 1) * ST] for g in range(SEGS)], axis=0
        )
        for t in range(per)
    ]
    spectra = dot(jnp.concatenate(lanes, axis=1).astype(bf16), dft)
    re, im = spectra[:, :NF], spectra[:, NF:]
    high, low = halves(jnp.sqrt(re * re + im * im))
    parts = dot(jnp.concatenate([high, low], axis=0), near)
    smooth = parts[: SEGS * ST] + parts[SEGS * ST :]
    factor = jnp.concatenate(masks, axis=0) / (smooth * (1.0 / (2 * WF + 1)) + 1e-06)
    return (re * factor).astype(bf16).astype(f32), (im * factor).astype(bf16).astype(f32)


def hour(ref):
    return [ref[h, :, 128 * i : 128 * (i + 1)].astype(f32) for h in range(2) for i in range(HALF // 128)]


def kernel(
    raw_hbm, mask_hbm, order_hbm, fir_hbm, box_hbm, dft_hbm, near_hbm, lag_hbm, out_ref,
    mask_ref, order_ref, fir_ref, box_ref, dft_ref, near_ref, lag_ref,
    own, own_mask, slots1, cand, slots2, picked, source, bulk,
    mslots1, mcand, mslots2, mpicked, source_mask, station, stack,
    copy_sem, pair_sem, mpair_sem, one_sem, two_sem, three_sem, mone_sem, mtwo_sem, mthree_sem,
):
    half = lax.axis_index("section")
    blk = lax.axis_index("blk")
    me = (blk // 16) * 2 + blk % 2
    x = (blk // 64) * 2 + half
    y = (blk // 16) % 4
    z = (blk // 2) % DEPTH
    core = blk % 2
    collects = x * y < 2
    late = x * y >= 2
    chip = x + y + 3 * ((y + 3) // 4) + 2 * x * y
    slot = jnp.where(collects, chip * 2 + core, PLANE)
    keeps_masks = half * N_BLK + blk == z * 2

    def device(chip, core):
        return (chip[0] % 2, (chip[0] // 2) * 64 + chip[1] * 16 + core + z * 2)

    collectors = [device(chip, i) for chip in CHIPS for i in range(2)]
    rest = [device(chip, i) for chip in REST for i in range(2)]

    def remote(src, dst, sems, to):
        return pltpu.make_async_remote_copy(
            src_ref=src, dst_ref=dst, send_sem=sems.at[0], recv_sem=sems.at[1],
            device_id=to, device_id_type=MESH,
        )

    def wait(ref, sem):
        pltpu.make_async_copy(ref, ref, sem).wait()

    def lanes(q):
        return pl.ds(q * PIECE if isinstance(q, int) else pl.multiple_of(q * PIECE, PIECE), PIECE)

    def above(depth):
        return (half, blk + (depth - z) * 2)

    other = (1 - half, blk)
    barrier = pltpu.get_barrier_semaphore()

    def signal(to):
        pl.semaphore_signal(barrier, inc=1, device_id=to, device_id_type=MESH)

    @pl.when(collects)
    def _():
        for to in rest:
            signal(to)

        for q, to in enumerate(collectors):

            @pl.when(slot != q)
            def _(to=to):
                signal(to)

        for depth in range(DEPTH):

            @pl.when(z != depth)
            def _(depth=depth):
                signal(above(depth))

    @pl.when(late)
    def _():
        signal(other)

    mine = own.at[half]
    copies = [
        pltpu.make_async_copy(src, dst, copy_sem.at[i])
        for i, (src, dst) in enumerate(
            (
                (raw_hbm, mine), (mask_hbm, mask_ref), (order_hbm, order_ref),
                (fir_hbm, fir_ref), (box_hbm, box_ref), (dft_hbm, dft_ref),
                (near_hbm, near_ref), (lag_hbm, lag_ref),
            )
        )
    ]
    for copy in copies:
        copy.start()
    copies[1].wait()
    flags = mask_ref[...].astype(f32)
    eye = lax.broadcasted_iota(jnp.int32, (ST, ST), 0) == lax.broadcasted_iota(
        jnp.int32, (ST, ST), 1
    )
    lane = lax.broadcasted_iota(jnp.int32, (ST, 128), 1)
    tile = jnp.zeros((ST, 128), f32)
    for g in range(SEG):
        row = jnp.where(eye, jnp.broadcast_to(flags[g : g + 1], (ST, ST)), 0.0)
        tile = jnp.where(lane == g, jnp.sum(row, axis=1, keepdims=True), tile)
    own_mask[half] = tile.astype(bf16)
    copies[0].wait()

    @pl.when(collects & (y < 2))
    def _():
        pl.semaphore_wait(barrier, DEPTH - 1 + PLANE - 1)

    @pl.when(collects & (y >= 2))
    def _():
        pl.semaphore_wait(barrier, DEPTH - 1 + PLANE)

    @pl.when(late & (x < 2))
    def _():
        pl.semaphore_wait(barrier, PLANE)

    @pl.when(late & (x >= 2))
    def _():
        pl.semaphore_wait(barrier, PLANE + 1)

    for q, to in enumerate(collectors):

        @pl.when(slot != q)
        def _(q=q, to=to):
            remote(own.at[half, :, lanes(q)], slots1.at[half, me], one_sem, to).start()

    pair = [
        remote(mine, mine, pair_sem, other),
        remote(own_mask.at[half], own_mask.at[half], mpair_sem, other),
    ]
    for copy in pair:
        copy.start()

    @pl.when(jnp.logical_not(keeps_masks))
    def _():
        remote(own_mask.at[half], mslots1.at[half, me], mone_sem, collectors[0]).start()

    copies[2].wait()
    root = [order_ref[i] for i in range(2)]
    root_plane = [(r // 16) * 2 + r % 2 for r in root]
    root_z = [(r // 2) % DEPTH for r in root]

    @pl.when(collects)
    def _():
        slots1[half, me] = own[half, :, lanes(slot)]
        wait(source.at[:, :, pl.ds(0, 31 * PIECE // 2)], one_sem.at[1])
        for i in range(2):
            for h in range(2):
                cand[i, h] = slots1[h, root_plane[i]]
        for depth in range(DEPTH):

            @pl.when(z != depth)
            def _(depth=depth):
                remote(cand, slots2.at[z], two_sem, above(depth)).start()

        slots2[z] = cand[...]

    @pl.when(keeps_masks)
    def _():
        mslots1[0, 0] = own_mask[0]
        wait(source.at[0, :, pl.ds(0, 31 * 128)], mone_sem.at[1])
        for i in range(2):
            for h in range(2):
                mcand[i, h] = mslots1[h, root_plane[i]]
        for depth in range(DEPTH):

            @pl.when(z != depth)
            def _(depth=depth):
                remote(mcand, mslots2.at[z], mtwo_sem, above(depth)).start()

        mslots2[z] = mcand[...]

    for copy in pair:
        copy.wait()
    for i in range(3, 7):
        copies[i].wait()
    weights = (fir_ref, box_ref, dft_ref, near_ref)
    masks = [own_mask[i].astype(f32) for i in range(2)]
    columns = [m[:, g : g + 1] for m in masks for g in range(SEG)]
    station[0], station[1] = whiten(hour(own), columns, *[w[...] for w in weights])

    @pl.when(collects)
    def _():
        wait(slots2.at[pl.ds(0, DEPTH - 1)], two_sem.at[1])
        for i in range(2):
            picked[i] = slots2[root_z[i], i]
        for q, to in enumerate(collectors):

            @pl.when(slot != q)
            def _(to=to):
                remote(picked.at[to[0]], source.at[:, :, lanes(slot)], three_sem, to).start()

        for to in rest:
            remote(picked.at[to[0]], source.at[:, :, lanes(slot)], three_sem, to).start()
        source[:, :, lanes(slot)] = picked[half]

    @pl.when(keeps_masks)
    def _():
        wait(mslots2.at[pl.ds(0, DEPTH - 1)], mtwo_sem.at[1])
        for i in range(2):
            mpicked[i] = mslots2[root_z[i], i]
        for to in collectors[1:] + rest:
            remote(mpicked.at[to[0]], source_mask, mthree_sem, to).start()
        source_mask[...] = mpicked[0]

    copies[7].wait()

    @pl.when(collects)
    def _():
        wait(source.at[:, :, pl.ds(0, 15 * PIECE)], three_sem.at[1])

    @pl.when(late)
    def _():
        wait(source, three_sem.at[1])

    @pl.when(jnp.logical_not(keeps_masks))
    def _():
        wait(source_mask, mthree_sem.at[1])

    theirs = [source_mask[i].astype(f32) for i in range(2)]
    columns = [m[:, g : g + 1] for m in theirs for g in range(SEG)]
    source_re, source_im = whiten(hour(source), columns, *[w[...] for w in weights])
    for k in range(KT):
        part = slice(128 * k, 128 * (k + 1))
        real = [jnp.zeros((ST, 128), f32)] * ST
        imag = [jnp.zeros((ST, 128), f32)] * ST
        for g in range(SEGS):
            re_s = station[0, ST * g : ST * (g + 1), part]
            im_s = station[1, ST * g : ST * (g + 1), part]
            for n in range(ST):
                re_n = source_re[ST * g + n : ST * g + n + 1, part]
                im_n = source_im[ST * g + n : ST * g + n + 1, part]
                real[n] = real[n] + (re_s * re_n + im_s * im_n)
                imag[n] = imag[n] + (im_s * re_n - re_s * im_n)
        for n in range(ST):
            stack[ST * n : ST * (n + 1), 128 * k : 128 * (k + 1)] = real[n]
            stack[ST * n : ST * (n + 1), NF + 128 * k : NF + 128 * (k + 1)] = imag[n]
    high, low = halves(stack[...])
    first = dot(high, lag_ref[...])
    lagged = first[:, :LAGS] + first[:, LAGS:] + dot(low, lag_ref[:, :LAGS])
    for n in range(ST):
        count = masks[0] * theirs[0][n : n + 1] + masks[1] * theirs[1][n : n + 1]
        count = jnp.maximum(jnp.sum(count, axis=1, keepdims=True), 1.0)
        out_ref[n] = lagged[ST * n : ST * (n + 1)] / count

    @pl.when(collects)
    def _():
        wait(source.at[0, :, pl.ds(0, 15 * PIECE)], one_sem.at[0])
        wait(slots2.at[pl.ds(0, DEPTH - 1)], two_sem.at[0])
        wait(bulk.at[pl.ds(0, 31)], three_sem.at[0])

    @pl.when(late)
    def _():
        wait(source.at[0], one_sem.at[0])

    @pl.when(keeps_masks)
    def _():
        wait(mslots2.at[pl.ds(0, DEPTH - 1)], mtwo_sem.at[0])
        wait(source.at[:, :, pl.ds(0, 31 * 128)], mthree_sem.at[0])

    @pl.when(jnp.logical_not(keeps_masks))
    def _():
        wait(own_mask.at[0], mone_sem.at[0])


def shards(raw_traces, valid_mask, block_order):
    constants = [jnp.asarray(t) for t in tables()]
    hbm = pl.BlockSpec(memory_space=pl.ANY)
    wide = (ST, PIECE)
    flag = (ST, 128)
    pair = pltpu.SemaphoreType.DMA((2,))
    return pl.pallas_call(
        kernel,
        out_shape=jax.ShapeDtypeStruct((ST, ST, LAGS), f32),
        in_specs=[hbm] * (3 + len(constants)),
        out_specs=pl.BlockSpec(memory_space=pltpu.VMEM),
        scratch_shapes=[
            pltpu.VMEM((SEG, ST), jnp.int32),
            pltpu.SMEM(block_order.shape, jnp.int32),
        ]
        + [pltpu.VMEM(c.shape, c.dtype) for c in constants]
        + [
            pltpu.VMEM((2, ST, HALF), bf16),
            pltpu.VMEM((2,) + flag, bf16),
            pltpu.VMEM((2, PLANE) + wide, bf16),
            pltpu.VMEM((2, 2) + wide, bf16),
            pltpu.VMEM((DEPTH, 2, 2) + wide, bf16),
            pltpu.VMEM((2, 2) + wide, bf16),
            pltpu.VMEM((2, ST, HALF), bf16),
            pltpu.VMEM((2 * PLANE, 2) + wide, bf16),
            pltpu.VMEM((2, PLANE) + flag, bf16),
            pltpu.VMEM((2, 2) + flag, bf16),
            pltpu.VMEM((DEPTH, 2, 2) + flag, bf16),
            pltpu.VMEM((2, 2) + flag, bf16),
            pltpu.VMEM((2,) + flag, bf16),
            pltpu.VMEM((2, SEGS * ST, NF), f32),
            pltpu.VMEM((ST * ST, 2 * NF), f32),
            pltpu.SemaphoreType.DMA((3 + len(constants),)),
            pair, pair, pair, pair, pair, pair, pair, pair,
        ],
        compiler_params=pltpu.CompilerParams(
            collective_id=0, has_side_effects=True, vmem_limit_bytes=VMEM_KIB << 10
        ),
    )(
        *[
            pltpu.with_memory_space_constraint(a, pltpu.HBM)
            for a in (raw_traces, valid_mask.T, block_order, *constants)
        ]
    )


def solution(mesh):
    return jax.shard_map(
        shards,
        mesh=mesh,
        in_specs=(P("blk", "section"), P("blk", "section"), P()),
        out_specs=P("section", "blk", None),
        check_vma=False,
    )
```

```python
import math

import jax
import jax.numpy as jnp
import ml_dtypes
import numpy as np
from jax import lax
from jax.experimental import pallas as pl
from jax.experimental.pallas import tpu as pltpu
from jax.sharding import PartitionSpec as P

L = 1024
NF = 384
BIN_LO = 8
LAGS = 256
TAPS = 33
HW = 50
WF = 32
KT = NF // 128
SEGS = 8
SEG = 4
HALF = SEG * L
ST = 8
PIECE = 256
VMEM_KIB = 32768
PLANE = 16
DEPTH = 8
N_BLK = 128
MESH = pl.DeviceIdType.MESH
CHIPS = [(x, 0) for x in range(4)] + [(0, y) for y in range(1, 4)] + [(1, 1)]
REST = [(1, 2), (2, 1), (3, 1), (2, 2), (3, 2), (1, 3), (2, 3), (3, 3)]
f32 = jnp.float32
bf16 = jnp.bfloat16


def split(values):
    high = values.astype(np.float32).astype(ml_dtypes.bfloat16)
    low = (values - high.astype(np.float64)).astype(ml_dtypes.bfloat16)
    return high, low


def tables():
    half = (TAPS - 1) // 2
    k = np.arange(-half, half + 1).astype(np.float64)
    a, b = BIN_LO / L, (BIN_LO + NF) / L
    taps = (0.5 + 0.5 * np.cos(2 * np.pi * k / (TAPS + 1))) * (
        2 * b * np.sinc(2 * b * k) - 2 * a * np.sinc(2 * a * k)
    )
    shift = np.arange(128)[None, :] + 128 - np.arange(384)[:, None]
    band = np.where(np.abs(shift) <= half, taps[np.clip(shift + half, 0, TAPS - 1)], 0.0)
    fir = np.concatenate(split(band), axis=1)
    apart = np.arange(256)[None, :] + 128 - np.arange(512)[:, None]
    box = (np.abs(apart) <= HW).astype(ml_dtypes.bfloat16)
    bins = BIN_LO + np.arange(NF)
    phase = (np.arange(L)[:, None] * bins[None, :]) % L * (2 * np.pi / L)
    dft = np.concatenate([np.cos(phase), -np.sin(phase)], axis=1)
    dft = dft.astype(np.float32).astype(ml_dtypes.bfloat16)
    near = np.abs(np.arange(NF)[:, None] - np.arange(NF)[None, :]) <= WF
    near = near.astype(ml_dtypes.bfloat16)
    phase = (bins[:, None] * (np.arange(LAGS) - LAGS // 2)[None, :]) % L * (2 * np.pi / L)
    lag = np.concatenate([np.cos(phase), -np.sin(phase)], axis=0) / math.sqrt(NF)
    lag = np.concatenate(split(lag), axis=1)
    return fir, box, dft, near, lag


def dot(a, b):
    return jnp.dot(a, b, preferred_element_type=f32)


def halves(x):
    high = x.astype(bf16)
    return high, (x - high.astype(f32)).astype(bf16)


def whiten(tiles, masks, fir, box, dft, near):
    zero = jnp.zeros((ST, 128), f32)
    edge = (len(tiles) + 2) * ST
    padded = [zero, zero] + tiles + [zero, zero]
    wide = jnp.concatenate(padded, axis=0).astype(bf16)
    mid = jnp.concatenate(padded[1:-1], axis=0).astype(bf16)
    both = dot(jnp.concatenate([wide[:edge], mid, wide[2 * ST :]], axis=1), fir)
    filtered = both[:, :128] + both[:, 128:]
    size = jnp.abs(filtered)
    count = len(tiles)
    around = [
        jnp.concatenate([size[ST * (i + j) : ST * (i + j + 1)] for j in range(0, count, 2)], axis=0)
        for i in range(4)
    ]
    window = dot(jnp.concatenate([a.astype(bf16) for a in around], axis=1), box)
    window = window * (1.0 / (2 * HW + 1)) + 1e-06
    normalized = [
        filtered[ST * (i + 1) : ST * (i + 2)]
        / window[ST * (i // 2) : ST * (i // 2 + 1), 128 * (i % 2) : 128 * (i % 2 + 1)]
        for i in range(count)
    ]
    per = L // 128
    lanes = [
        jnp.concatenate(
            [normalized[g * per + t] for g in range(SEGS)], axis=0
        )
        for t in range(per)
    ]
    spectra = dot(jnp.concatenate(lanes, axis=1).astype(bf16), dft)
    re, im = spectra[:, :NF], spectra[:, NF:]
    high, low = halves(jnp.sqrt(re * re + im * im))
    parts = dot(jnp.concatenate([high, low], axis=0), near)
    smooth = parts[: SEGS * ST] + parts[SEGS * ST :]
    factor = jnp.concatenate(masks, axis=0) / (smooth * (1.0 / (2 * WF + 1)) + 1e-06)
    return (re * factor).astype(bf16).astype(f32), (im * factor).astype(bf16).astype(f32)


def hour(ref):
    return [ref[h, :, 128 * i : 128 * (i + 1)].astype(f32) for h in range(2) for i in range(HALF // 128)]


def kernel(
    raw_hbm, mask_hbm, order_hbm, fir_hbm, box_hbm, dft_hbm, near_hbm, lag_hbm, out_ref,
    mask_ref, order_ref, fir_ref, box_ref, dft_ref, near_ref, lag_ref,
    own, own_mask, slots1, cand, slots2, picked, source, bulk,
    mslots1, mcand, mslots2, mpicked, source_mask, station, stack,
    copy_sem, pair_sem, mpair_sem, one_sem, two_sem, three_sem, mone_sem, mtwo_sem, mthree_sem,
):
    half = lax.axis_index("section")
    blk = lax.axis_index("blk")
    me = (blk // 16) * 2 + blk % 2
    x = (blk // 64) * 2 + half
    y = (blk // 16) % 4
    z = (blk // 2) % DEPTH
    core = blk % 2
    collects = x * y < 2
    late = x * y >= 2
    chip = x + y + 3 * ((y + 3) // 4) + 2 * x * y
    slot = jnp.where(collects, chip * 2 + core, PLANE)
    keeps_masks = half * N_BLK + blk == z * 2

    def device(chip, core):
        return (chip[0] % 2, (chip[0] // 2) * 64 + chip[1] * 16 + core + z * 2)

    collectors = [device(chip, i) for chip in CHIPS for i in range(2)]
    rest = [device(chip, i) for chip in REST for i in range(2)]

    def remote(src, dst, sems, to):
        return pltpu.make_async_remote_copy(
            src_ref=src, dst_ref=dst, send_sem=sems.at[0], recv_sem=sems.at[1],
            device_id=to, device_id_type=MESH,
        )

    def wait(ref, sem):
        pltpu.make_async_copy(ref, ref, sem).wait()

    def lanes(q):
        return pl.ds(q * PIECE if isinstance(q, int) else pl.multiple_of(q * PIECE, PIECE), PIECE)

    def above(depth):
        return (half, blk + (depth - z) * 2)

    other = (1 - half, blk)
    barrier = pltpu.get_barrier_semaphore()

    def signal(to):
        pl.semaphore_signal(barrier, inc=1, device_id=to, device_id_type=MESH)

    @pl.when(collects)
    def _():
        for to in rest:
            signal(to)

        for q, to in enumerate(collectors):

            @pl.when(slot != q)
            def _(to=to):
                signal(to)

        for depth in range(DEPTH):

            @pl.when(z != depth)
            def _(depth=depth):
                signal(above(depth))

    @pl.when(late)
    def _():
        signal(other)

    mine = own.at[half]
    copies = [
        pltpu.make_async_copy(src, dst, copy_sem.at[i])
        for i, (src, dst) in enumerate(
            (
                (raw_hbm, mine), (mask_hbm, mask_ref), (order_hbm, order_ref),
                (fir_hbm, fir_ref), (box_hbm, box_ref), (dft_hbm, dft_ref),
                (near_hbm, near_ref), (lag_hbm, lag_ref),
            )
        )
    ]
    for copy in copies:
        copy.start()
    copies[1].wait()
    flags = mask_ref[...].astype(f32)
    eye = lax.broadcasted_iota(jnp.int32, (ST, ST), 0) == lax.broadcasted_iota(
        jnp.int32, (ST, ST), 1
    )
    lane = lax.broadcasted_iota(jnp.int32, (ST, 128), 1)
    tile = jnp.zeros((ST, 128), f32)
    for g in range(SEG):
        row = jnp.where(eye, jnp.broadcast_to(flags[g : g + 1], (ST, ST)), 0.0)
        tile = jnp.where(lane == g, jnp.sum(row, axis=1, keepdims=True), tile)
    own_mask[half] = tile.astype(bf16)
    copies[0].wait()

    @pl.when(collects & (y < 2))
    def _():
        pl.semaphore_wait(barrier, DEPTH - 1 + PLANE - 1)

    @pl.when(collects & (y >= 2))
    def _():
        pl.semaphore_wait(barrier, DEPTH - 1 + PLANE)

    @pl.when(late & (x < 2))
    def _():
        pl.semaphore_wait(barrier, PLANE)

    @pl.when(late & (x >= 2))
    def _():
        pl.semaphore_wait(barrier, PLANE + 1)

    for q, to in enumerate(collectors):

        @pl.when(slot != q)
        def _(q=q, to=to):
            remote(own.at[half, :, lanes(q)], slots1.at[half, me], one_sem, to).start()

    pair = [
        remote(mine, mine, pair_sem, other),
        remote(own_mask.at[half], own_mask.at[half], mpair_sem, other),
    ]
    for copy in pair:
        copy.start()

    @pl.when(jnp.logical_not(keeps_masks))
    def _():
        remote(own_mask.at[half], mslots1.at[half, me], mone_sem, collectors[0]).start()

    copies[2].wait()
    root = [order_ref[i] for i in range(2)]
    root_plane = [(r // 16) * 2 + r % 2 for r in root]
    root_z = [(r // 2) % DEPTH for r in root]

    @pl.when(collects)
    def _():
        slots1[half, me] = own[half, :, lanes(slot)]
        wait(source.at[:, :, pl.ds(0, 31 * PIECE // 2)], one_sem.at[1])
        for i in range(2):
            for h in range(2):
                cand[i, h] = slots1[h, root_plane[i]]
        for depth in range(DEPTH):

            @pl.when(z != depth)
            def _(depth=depth):
                remote(cand, slots2.at[z], two_sem, above(depth)).start()

        slots2[z] = cand[...]

    @pl.when(keeps_masks)
    def _():
        mslots1[0, 0] = own_mask[0]
        wait(source.at[0, :, pl.ds(0, 31 * 128)], mone_sem.at[1])
        for i in range(2):
            for h in range(2):
                mcand[i, h] = mslots1[h, root_plane[i]]
        for depth in range(DEPTH):

            @pl.when(z != depth)
            def _(depth=depth):
                remote(mcand, mslots2.at[z], mtwo_sem, above(depth)).start()

        mslots2[z] = mcand[...]

    for copy in pair:
        copy.wait()
    for i in range(3, 7):
        copies[i].wait()
    weights = (fir_ref, box_ref, dft_ref, near_ref)
    masks = [own_mask[i].astype(f32) for i in range(2)]
    columns = [m[:, g : g + 1] for m in masks for g in range(SEG)]
    station[0], station[1] = whiten(hour(own), columns, *[w[...] for w in weights])

    @pl.when(collects)
    def _():
        wait(slots2.at[pl.ds(0, DEPTH - 1)], two_sem.at[1])
        for i in range(2):
            picked[i] = slots2[root_z[i], i]
        for q, to in enumerate(collectors):

            @pl.when(slot != q)
            def _(to=to):
                remote(picked.at[to[0]], source.at[:, :, lanes(slot)], three_sem, to).start()

        for to in rest:
            remote(picked.at[to[0]], source.at[:, :, lanes(slot)], three_sem, to).start()
        source[:, :, lanes(slot)] = picked[half]

    @pl.when(keeps_masks)
    def _():
        wait(mslots2.at[pl.ds(0, DEPTH - 1)], mtwo_sem.at[1])
        for i in range(2):
            mpicked[i] = mslots2[root_z[i], i]
        for to in collectors[1:] + rest:
            remote(mpicked.at[to[0]], source_mask, mthree_sem, to).start()
        source_mask[...] = mpicked[0]

    copies[7].wait()

    @pl.when(collects)
    def _():
        wait(source.at[:, :, pl.ds(0, 15 * PIECE)], three_sem.at[1])

    @pl.when(late)
    def _():
        wait(source, three_sem.at[1])

    @pl.when(jnp.logical_not(keeps_masks))
    def _():
        wait(source_mask, mthree_sem.at[1])

    theirs = [source_mask[i].astype(f32) for i in range(2)]
    columns = [m[:, g : g + 1] for m in theirs for g in range(SEG)]
    source_re, source_im = whiten(hour(source), columns, *[w[...] for w in weights])
    for k in range(KT):
        part = slice(128 * k, 128 * (k + 1))
        real = [jnp.zeros((ST, 128), f32)] * ST
        imag = [jnp.zeros((ST, 128), f32)] * ST
        for g in range(SEGS):
            re_s = station[0, ST * g : ST * (g + 1), part]
            im_s = station[1, ST * g : ST * (g + 1), part]
            for n in range(ST):
                re_n = source_re[ST * g + n : ST * g + n + 1, part]
                im_n = source_im[ST * g + n : ST * g + n + 1, part]
                real[n] = real[n] + (re_s * re_n + im_s * im_n)
                imag[n] = imag[n] + (im_s * re_n - re_s * im_n)
        for n in range(ST):
            stack[ST * n : ST * (n + 1), 128 * k : 128 * (k + 1)] = real[n]
            stack[ST * n : ST * (n + 1), NF + 128 * k : NF + 128 * (k + 1)] = imag[n]
    high, low = halves(stack[...])
    first = dot(high, lag_ref[...])
    lagged = first[:, :LAGS] + first[:, LAGS:] + dot(low, lag_ref[:, :LAGS])
    for n in range(ST):
        count = masks[0] * theirs[0][n : n + 1] + masks[1] * theirs[1][n : n + 1]
        count = jnp.maximum(jnp.sum(count, axis=1, keepdims=True), 1.0)
        out_ref[n] = lagged[ST * n : ST * (n + 1)] / count

    @pl.when(collects)
    def _():
        wait(source.at[0, :, pl.ds(0, 15 * PIECE)], one_sem.at[0])
        wait(slots2.at[pl.ds(0, DEPTH - 1)], two_sem.at[0])
        wait(bulk.at[pl.ds(0, 31)], three_sem.at[0])

    @pl.when(late)
    def _():
        wait(source.at[0], one_sem.at[0])

    @pl.when(keeps_masks)
    def _():
        wait(mslots2.at[pl.ds(0, DEPTH - 1)], mtwo_sem.at[0])
        wait(source.at[:, :, pl.ds(0, 31 * 128)], mthree_sem.at[0])

    @pl.when(jnp.logical_not(keeps_masks))
    def _():
        wait(own_mask.at[0], mone_sem.at[0])


def shards(raw_traces, valid_mask, block_order):
    constants = [jnp.asarray(t) for t in tables()]
    hbm = pl.BlockSpec(memory_space=pl.ANY)
    wide = (ST, PIECE)
    flag = (ST, 128)
    pair = pltpu.SemaphoreType.DMA((2,))
    return pl.pallas_call(
        kernel,
        out_shape=jax.ShapeDtypeStruct((ST, ST, LAGS), f32),
        in_specs=[hbm] * (3 + len(constants)),
        out_specs=pl.BlockSpec(memory_space=pltpu.VMEM),
        scratch_shapes=[
            pltpu.VMEM((SEG, ST), jnp.int32),
            pltpu.SMEM(block_order.shape, jnp.int32),
        ]
        + [pltpu.VMEM(c.shape, c.dtype) for c in constants]
        + [
            pltpu.VMEM((2, ST, HALF), bf16),
            pltpu.VMEM((2,) + flag, bf16),
            pltpu.VMEM((2, PLANE) + wide, bf16),
            pltpu.VMEM((2, 2) + wide, bf16),
            pltpu.VMEM((DEPTH, 2, 2) + wide, bf16),
            pltpu.VMEM((2, 2) + wide, bf16),
            pltpu.VMEM((2, ST, HALF), bf16),
            pltpu.VMEM((2 * PLANE, 2) + wide, bf16),
            pltpu.VMEM((2, PLANE) + flag, bf16),
            pltpu.VMEM((2, 2) + flag, bf16),
            pltpu.VMEM((DEPTH, 2, 2) + flag, bf16),
            pltpu.VMEM((2, 2) + flag, bf16),
            pltpu.VMEM((2,) + flag, bf16),
            pltpu.VMEM((2, SEGS * ST, NF), f32),
            pltpu.VMEM((ST * ST, 2 * NF), f32),
            pltpu.SemaphoreType.DMA((3 + len(constants),)),
            pair, pair, pair, pair, pair, pair, pair, pair,
        ],
        compiler_params=pltpu.CompilerParams(
            collective_id=0, has_side_effects=True, vmem_limit_bytes=VMEM_KIB << 10
        ),
    )(
        *[
            pltpu.with_memory_space_constraint(a, pltpu.HBM)
            for a in (raw_traces, valid_mask.T, block_order, *constants)
        ]
    )


def solution(mesh):
    return jax.shard_map(
        shards,
        mesh=mesh,
        in_specs=(P("blk", "section"), P("blk", "section"), P()),
        out_specs=P("section", "blk", None),
        check_vma=False,
    )
```

```python
import math

import jax
import jax.numpy as jnp
import ml_dtypes
import numpy as np
from jax import lax
from jax.experimental import pallas as pl
from jax.experimental.pallas import tpu as pltpu
from jax.sharding import PartitionSpec as P

L = 1024
NF = 384
BIN_LO = 8
LAGS = 256
TAPS = 33
HW = 50
WF = 32
KT = NF // 128
SEGS = 8
SEG = 4
HALF = SEG * L
ST = 8
PIECE = 256
VMEM_KIB = 32768
PLANE = 16
DEPTH = 8
N_BLK = 128
MESH = pl.DeviceIdType.MESH
CHIPS = [(x, 0) for x in range(4)] + [(0, y) for y in range(1, 4)] + [(1, 1)]
REST = [(1, 2), (2, 1), (3, 1), (2, 2), (3, 2), (1, 3), (2, 3), (3, 3)]
f32 = jnp.float32
bf16 = jnp.bfloat16


def split(values):
    high = values.astype(np.float32).astype(ml_dtypes.bfloat16)
    low = (values - high.astype(np.float64)).astype(ml_dtypes.bfloat16)
    return high, low


def tables():
    half = (TAPS - 1) // 2
    k = np.arange(-half, half + 1).astype(np.float64)
    a, b = BIN_LO / L, (BIN_LO + NF) / L
    taps = (0.5 + 0.5 * np.cos(2 * np.pi * k / (TAPS + 1))) * (
        2 * b * np.sinc(2 * b * k) - 2 * a * np.sinc(2 * a * k)
    )
    shift = np.arange(128)[None, :] + 128 - np.arange(384)[:, None]
    band = np.where(np.abs(shift) <= half, taps[np.clip(shift + half, 0, TAPS - 1)], 0.0)
    fir = np.concatenate(split(band), axis=1)
    apart = np.arange(256)[None, :] + 128 - np.arange(512)[:, None]
    box = (np.abs(apart) <= HW).astype(ml_dtypes.bfloat16)
    bins = BIN_LO + np.arange(NF)
    phase = (np.arange(L)[:, None] * bins[None, :]) % L * (2 * np.pi / L)
    dft = np.concatenate([np.cos(phase), -np.sin(phase)], axis=1)
    dft = dft.astype(np.float32).astype(ml_dtypes.bfloat16)
    near = np.abs(np.arange(NF)[:, None] - np.arange(NF)[None, :]) <= WF
    near = near.astype(ml_dtypes.bfloat16)
    phase = (bins[:, None] * (np.arange(LAGS) - LAGS // 2)[None, :]) % L * (2 * np.pi / L)
    lag = np.concatenate([np.cos(phase), -np.sin(phase)], axis=0) / math.sqrt(NF)
    lag = np.concatenate(split(lag), axis=1)
    return fir, box, dft, near, lag


def dot(a, b):
    return jnp.dot(a, b, preferred_element_type=f32)


def halves(x):
    high = x.astype(bf16)
    return high, (x - high.astype(f32)).astype(bf16)


def whiten(tiles, masks, fir, box, dft, near):
    zero = jnp.zeros((ST, 128), f32)
    edge = (len(tiles) + 2) * ST
    padded = [zero, zero] + tiles + [zero, zero]
    wide = jnp.concatenate(padded, axis=0).astype(bf16)
    mid = jnp.concatenate(padded[1:-1], axis=0).astype(bf16)
    both = dot(jnp.concatenate([wide[:edge], mid, wide[2 * ST :]], axis=1), fir)
    filtered = both[:, :128] + both[:, 128:]
    size = jnp.abs(filtered)
    count = len(tiles)
    around = [
        jnp.concatenate([size[ST * (i + j) : ST * (i + j + 1)] for j in range(0, count, 2)], axis=0)
        for i in range(4)
    ]
    window = dot(jnp.concatenate([a.astype(bf16) for a in around], axis=1), box)
    window = window * (1.0 / (2 * HW + 1)) + 1e-06
    normalized = [
        filtered[ST * (i + 1) : ST * (i + 2)]
        / window[ST * (i // 2) : ST * (i // 2 + 1), 128 * (i % 2) : 128 * (i % 2 + 1)]
        for i in range(count)
    ]
    per = L // 128
    lanes = [
        jnp.concatenate(
            [normalized[g * per + t] for g in range(SEGS)], axis=0
        )
        for t in range(per)
    ]
    spectra = dot(jnp.concatenate(lanes, axis=1).astype(bf16), dft)
    re, im = spectra[:, :NF], spectra[:, NF:]
    high, low = halves(jnp.sqrt(re * re + im * im))
    parts = dot(jnp.concatenate([high, low], axis=0), near)
    smooth = parts[: SEGS * ST] + parts[SEGS * ST :]
    factor = jnp.concatenate(masks, axis=0) / (smooth * (1.0 / (2 * WF + 1)) + 1e-06)
    return (re * factor).astype(bf16).astype(f32), (im * factor).astype(bf16).astype(f32)


def hour(ref):
    return [ref[h, :, 128 * i : 128 * (i + 1)].astype(f32) for h in range(2) for i in range(HALF // 128)]


def kernel(
    raw_hbm, mask_hbm, order_hbm, fir_hbm, box_hbm, dft_hbm, near_hbm, lag_hbm, out_ref,
    mask_ref, order_ref, fir_ref, box_ref, dft_ref, near_ref, lag_ref,
    own, own_mask, slots1, cand, slots2, picked, source, bulk,
    mslots1, mcand, mslots2, mpicked, source_mask, station, stack,
    copy_sem, pair_sem, mpair_sem, one_sem, two_sem, three_sem, mone_sem, mtwo_sem, mthree_sem,
):
    half = lax.axis_index("section")
    blk = lax.axis_index("blk")
    me = (blk // 16) * 2 + blk % 2
    x = (blk // 64) * 2 + half
    y = (blk // 16) % 4
    z = (blk // 2) % DEPTH
    core = blk % 2
    collects = x * y < 2
    late = x * y >= 2
    chip = x + y + 3 * ((y + 3) // 4) + 2 * x * y
    slot = jnp.where(collects, chip * 2 + core, PLANE)
    keeps_masks = half * N_BLK + blk == z * 2

    def device(chip, core):
        return (chip[0] % 2, (chip[0] // 2) * 64 + chip[1] * 16 + core + z * 2)

    collectors = [device(chip, i) for chip in CHIPS for i in range(2)]
    rest = [device(chip, i) for chip in REST for i in range(2)]

    def remote(src, dst, sems, to):
        return pltpu.make_async_remote_copy(
            src_ref=src, dst_ref=dst, send_sem=sems.at[0], recv_sem=sems.at[1],
            device_id=to, device_id_type=MESH,
        )

    def wait(ref, sem):
        pltpu.make_async_copy(ref, ref, sem).wait()

    def lanes(q):
        return pl.ds(q * PIECE if isinstance(q, int) else pl.multiple_of(q * PIECE, PIECE), PIECE)

    def above(depth):
        return (half, blk + (depth - z) * 2)

    other = (1 - half, blk)
    barrier = pltpu.get_barrier_semaphore()

    def signal(to):
        pl.semaphore_signal(barrier, inc=1, device_id=to, device_id_type=MESH)

    @pl.when(collects)
    def _():
        for to in rest:
            signal(to)

        for q, to in enumerate(collectors):

            @pl.when(slot != q)
            def _(to=to):
                signal(to)

        for depth in range(DEPTH):

            @pl.when(z != depth)
            def _(depth=depth):
                signal(above(depth))

    @pl.when(late)
    def _():
        signal(other)

    mine = own.at[half]
    copies = [
        pltpu.make_async_copy(src, dst, copy_sem.at[i])
        for i, (src, dst) in enumerate(
            (
                (raw_hbm, mine), (mask_hbm, mask_ref), (order_hbm, order_ref),
                (fir_hbm, fir_ref), (box_hbm, box_ref), (dft_hbm, dft_ref),
                (near_hbm, near_ref), (lag_hbm, lag_ref),
            )
        )
    ]
    for copy in copies:
        copy.start()
    copies[1].wait()
    flags = mask_ref[...].astype(f32)
    eye = lax.broadcasted_iota(jnp.int32, (ST, ST), 0) == lax.broadcasted_iota(
        jnp.int32, (ST, ST), 1
    )
    lane = lax.broadcasted_iota(jnp.int32, (ST, 128), 1)
    tile = jnp.zeros((ST, 128), f32)
    for g in range(SEG):
        row = jnp.where(eye, jnp.broadcast_to(flags[g : g + 1], (ST, ST)), 0.0)
        tile = jnp.where(lane == g, jnp.sum(row, axis=1, keepdims=True), tile)
    own_mask[half] = tile.astype(bf16)
    copies[0].wait()

    @pl.when(collects & (y < 2))
    def _():
        pl.semaphore_wait(barrier, DEPTH - 1 + PLANE - 1)

    @pl.when(collects & (y >= 2))
    def _():
        pl.semaphore_wait(barrier, DEPTH - 1 + PLANE)

    @pl.when(late & (x < 2))
    def _():
        pl.semaphore_wait(barrier, PLANE)

    @pl.when(late & (x >= 2))
    def _():
        pl.semaphore_wait(barrier, PLANE + 1)

    for q, to in enumerate(collectors):

        @pl.when(slot != q)
        def _(q=q, to=to):
            remote(own.at[half, :, lanes(q)], slots1.at[half, me], one_sem, to).start()

    pair = [
        remote(mine, mine, pair_sem, other),
        remote(own_mask.at[half], own_mask.at[half], mpair_sem, other),
    ]
    for copy in pair:
        copy.start()

    @pl.when(jnp.logical_not(keeps_masks))
    def _():
        remote(own_mask.at[half], mslots1.at[half, me], mone_sem, collectors[0]).start()

    copies[2].wait()
    root = [order_ref[i] for i in range(2)]
    root_plane = [(r // 16) * 2 + r % 2 for r in root]
    root_z = [(r // 2) % DEPTH for r in root]

    @pl.when(collects)
    def _():
        slots1[half, me] = own[half, :, lanes(slot)]
        wait(source.at[:, :, pl.ds(0, 31 * PIECE // 2)], one_sem.at[1])
        for i in range(2):
            for h in range(2):
                cand[i, h] = slots1[h, root_plane[i]]
        for depth in range(DEPTH):

            @pl.when(z != depth)
            def _(depth=depth):
                remote(cand, slots2.at[z], two_sem, above(depth)).start()

        slots2[z] = cand[...]

    @pl.when(keeps_masks)
    def _():
        mslots1[0, 0] = own_mask[0]
        wait(source.at[0, :, pl.ds(0, 31 * 128)], mone_sem.at[1])
        for i in range(2):
            for h in range(2):
                mcand[i, h] = mslots1[h, root_plane[i]]
        for depth in range(DEPTH):

            @pl.when(z != depth)
            def _(depth=depth):
                remote(mcand, mslots2.at[z], mtwo_sem, above(depth)).start()

        mslots2[z] = mcand[...]

    for copy in pair:
        copy.wait()
    for i in range(3, 7):
        copies[i].wait()
    weights = (fir_ref, box_ref, dft_ref, near_ref)
    masks = [own_mask[i].astype(f32) for i in range(2)]
    columns = [m[:, g : g + 1] for m in masks for g in range(SEG)]
    station[0], station[1] = whiten(hour(own), columns, *[w[...] for w in weights])

    @pl.when(collects)
    def _():
        wait(slots2.at[pl.ds(0, DEPTH - 1)], two_sem.at[1])
        for i in range(2):
            picked[i] = slots2[root_z[i], i]
        for q, to in enumerate(collectors):

            @pl.when(slot != q)
            def _(to=to):
                remote(picked.at[to[0]], source.at[:, :, lanes(slot)], three_sem, to).start()

        for to in rest:
            remote(picked.at[to[0]], source.at[:, :, lanes(slot)], three_sem, to).start()
        source[:, :, lanes(slot)] = picked[half]

    @pl.when(keeps_masks)
    def _():
        wait(mslots2.at[pl.ds(0, DEPTH - 1)], mtwo_sem.at[1])
        for i in range(2):
            mpicked[i] = mslots2[root_z[i], i]
        for to in collectors[1:] + rest:
            remote(mpicked.at[to[0]], source_mask, mthree_sem, to).start()
        source_mask[...] = mpicked[0]

    copies[7].wait()

    @pl.when(collects)
    def _():
        wait(source.at[:, :, pl.ds(0, 15 * PIECE)], three_sem.at[1])

    @pl.when(late)
    def _():
        wait(source, three_sem.at[1])

    @pl.when(jnp.logical_not(keeps_masks))
    def _():
        wait(source_mask, mthree_sem.at[1])

    theirs = [source_mask[i].astype(f32) for i in range(2)]
    columns = [m[:, g : g + 1] for m in theirs for g in range(SEG)]
    source_re, source_im = whiten(hour(source), columns, *[w[...] for w in weights])
    for k in range(KT):
        part = slice(128 * k, 128 * (k + 1))
        real = [jnp.zeros((ST, 128), f32)] * ST
        imag = [jnp.zeros((ST, 128), f32)] * ST
        for g in range(SEGS):
            re_s = station[0, ST * g : ST * (g + 1), part]
            im_s = station[1, ST * g : ST * (g + 1), part]
            for n in range(ST):
                re_n = source_re[ST * g + n : ST * g + n + 1, part]
                im_n = source_im[ST * g + n : ST * g + n + 1, part]
                real[n] = real[n] + (re_s * re_n + im_s * im_n)
                imag[n] = imag[n] + (im_s * re_n - re_s * im_n)
        for n in range(ST):
            stack[ST * n : ST * (n + 1), 128 * k : 128 * (k + 1)] = real[n]
            stack[ST * n : ST * (n + 1), NF + 128 * k : NF + 128 * (k + 1)] = imag[n]
    high, low = halves(stack[...])
    parts = dot(jnp.concatenate([high, low], axis=0), lag_ref[...])
    upper = parts[: ST * ST]
    lagged = upper[:, :LAGS] + upper[:, LAGS:] + parts[ST * ST :, :LAGS]
    for n in range(ST):
        count = masks[0] * theirs[0][n : n + 1] + masks[1] * theirs[1][n : n + 1]
        count = jnp.maximum(jnp.sum(count, axis=1, keepdims=True), 1.0)
        out_ref[n] = lagged[ST * n : ST * (n + 1)] / count

    @pl.when(collects)
    def _():
        wait(source.at[0, :, pl.ds(0, 15 * PIECE)], one_sem.at[0])
        wait(slots2.at[pl.ds(0, DEPTH - 1)], two_sem.at[0])
        wait(bulk.at[pl.ds(0, 31)], three_sem.at[0])

    @pl.when(late)
    def _():
        wait(source.at[0], one_sem.at[0])

    @pl.when(keeps_masks)
    def _():
        wait(mslots2.at[pl.ds(0, DEPTH - 1)], mtwo_sem.at[0])
        wait(source.at[:, :, pl.ds(0, 31 * 128)], mthree_sem.at[0])

    @pl.when(jnp.logical_not(keeps_masks))
    def _():
        wait(own_mask.at[0], mone_sem.at[0])


def shards(raw_traces, valid_mask, block_order):
    constants = [jnp.asarray(t) for t in tables()]
    hbm = pl.BlockSpec(memory_space=pl.ANY)
    wide = (ST, PIECE)
    flag = (ST, 128)
    pair = pltpu.SemaphoreType.DMA((2,))
    return pl.pallas_call(
        kernel,
        out_shape=jax.ShapeDtypeStruct((ST, ST, LAGS), f32),
        in_specs=[hbm] * (3 + len(constants)),
        out_specs=pl.BlockSpec(memory_space=pltpu.VMEM),
        scratch_shapes=[
            pltpu.VMEM((SEG, ST), jnp.int32),
            pltpu.SMEM(block_order.shape, jnp.int32),
        ]
        + [pltpu.VMEM(c.shape, c.dtype) for c in constants]
        + [
            pltpu.VMEM((2, ST, HALF), bf16),
            pltpu.VMEM((2,) + flag, bf16),
            pltpu.VMEM((2, PLANE) + wide, bf16),
            pltpu.VMEM((2, 2) + wide, bf16),
            pltpu.VMEM((DEPTH, 2, 2) + wide, bf16),
            pltpu.VMEM((2, 2) + wide, bf16),
            pltpu.VMEM((2, ST, HALF), bf16),
            pltpu.VMEM((2 * PLANE, 2) + wide, bf16),
            pltpu.VMEM((2, PLANE) + flag, bf16),
            pltpu.VMEM((2, 2) + flag, bf16),
            pltpu.VMEM((DEPTH, 2, 2) + flag, bf16),
            pltpu.VMEM((2, 2) + flag, bf16),
            pltpu.VMEM((2,) + flag, bf16),
            pltpu.VMEM((2, SEGS * ST, NF), f32),
            pltpu.VMEM((ST * ST, 2 * NF), f32),
            pltpu.SemaphoreType.DMA((3 + len(constants),)),
            pair, pair, pair, pair, pair, pair, pair, pair,
        ],
        compiler_params=pltpu.CompilerParams(
            collective_id=0, has_side_effects=True, vmem_limit_bytes=VMEM_KIB << 10
        ),
    )(
        *[
            pltpu.with_memory_space_constraint(a, pltpu.HBM)
            for a in (raw_traces, valid_mask.T, block_order, *constants)
        ]
    )


def solution(mesh):
    return jax.shard_map(
        shards,
        mesh=mesh,
        in_specs=(P("blk", "section"), P("blk", "section"), P()),
        out_specs=P("section", "blk", None),
        check_vma=False,
    )
```

```python
import math

import jax
import jax.numpy as jnp
import ml_dtypes
import numpy as np
from jax import lax
from jax.experimental import pallas as pl
from jax.experimental.pallas import tpu as pltpu
from jax.sharding import PartitionSpec as P

L = 1024
NF = 384
BIN_LO = 8
LAGS = 256
TAPS = 33
HW = 50
WF = 32
KT = NF // 128
SEGS = 8
SEG = 4
HALF = SEG * L
ST = 8
PIECE = 256
VMEM_KIB = 32768
PLANE = 16
DEPTH = 8
N_BLK = 128
MESH = pl.DeviceIdType.MESH
CHIPS = [(x, 0) for x in range(4)] + [(0, y) for y in range(1, 4)] + [(1, 1)]
REST = [(1, 2), (2, 1), (3, 1), (2, 2), (3, 2), (1, 3), (2, 3), (3, 3)]
f32 = jnp.float32
bf16 = jnp.bfloat16


def split(values):
    high = values.astype(np.float32).astype(ml_dtypes.bfloat16)
    low = (values - high.astype(np.float64)).astype(ml_dtypes.bfloat16)
    return high, low


def tables():
    half = (TAPS - 1) // 2
    k = np.arange(-half, half + 1).astype(np.float64)
    a, b = BIN_LO / L, (BIN_LO + NF) / L
    taps = (0.5 + 0.5 * np.cos(2 * np.pi * k / (TAPS + 1))) * (
        2 * b * np.sinc(2 * b * k) - 2 * a * np.sinc(2 * a * k)
    )
    shift = np.arange(128)[None, :] + 128 - np.arange(384)[:, None]
    band = np.where(np.abs(shift) <= half, taps[np.clip(shift + half, 0, TAPS - 1)], 0.0)
    fir = np.concatenate(split(band), axis=1)
    apart = np.arange(256)[None, :] + 128 - np.arange(512)[:, None]
    box = (np.abs(apart) <= HW).astype(ml_dtypes.bfloat16)
    bins = BIN_LO + np.arange(NF)
    phase = (np.arange(L)[:, None] * bins[None, :]) % L * (2 * np.pi / L)
    dft = np.concatenate([np.cos(phase), -np.sin(phase)], axis=1)
    dft = dft.astype(np.float32).astype(ml_dtypes.bfloat16)
    near = np.abs(np.arange(NF)[:, None] - np.arange(NF)[None, :]) <= WF
    near = near.astype(ml_dtypes.bfloat16)
    phase = (bins[:, None] * (np.arange(LAGS) - LAGS // 2)[None, :]) % L * (2 * np.pi / L)
    lag = np.concatenate([np.cos(phase), -np.sin(phase)], axis=0) / math.sqrt(NF)
    lag = np.concatenate(split(lag), axis=1)
    return fir, box, dft, near, lag


def dot(a, b):
    return jnp.dot(a, b, preferred_element_type=f32)


def halves(x):
    high = x.astype(bf16)
    return high, (x - high.astype(f32)).astype(bf16)


def whiten(tiles, masks, fir, box, dft, near):
    zero = jnp.zeros((ST, 128), f32)
    edge = (len(tiles) + 2) * ST
    padded = [zero, zero] + tiles + [zero, zero]
    wide = jnp.concatenate(padded, axis=0).astype(bf16)
    mid = jnp.concatenate(padded[1:-1], axis=0).astype(bf16)
    both = dot(jnp.concatenate([wide[:edge], mid, wide[2 * ST :]], axis=1), fir)
    filtered = both[:, :128] + both[:, 128:]
    size = jnp.abs(filtered)
    count = len(tiles)
    around = [
        jnp.concatenate([size[ST * (i + j) : ST * (i + j + 1)] for j in range(0, count, 2)], axis=0)
        for i in range(4)
    ]
    window = dot(jnp.concatenate([a.astype(bf16) for a in around], axis=1), box)
    window = window * (1.0 / (2 * HW + 1)) + 1e-06
    normalized = [
        filtered[ST * (i + 1) : ST * (i + 2)]
        / window[ST * (i // 2) : ST * (i // 2 + 1), 128 * (i % 2) : 128 * (i % 2 + 1)]
        for i in range(count)
    ]
    per = L // 128
    lanes = [
        jnp.concatenate(
            [normalized[g * per + t] for g in range(SEGS)], axis=0
        )
        for t in range(per)
    ]
    spectra = dot(jnp.concatenate(lanes, axis=1).astype(bf16), dft)
    re, im = spectra[:, :NF], spectra[:, NF:]
    high, low = halves(jnp.sqrt(re * re + im * im))
    parts = dot(jnp.concatenate([high, low], axis=0), near)
    smooth = parts[: SEGS * ST] + parts[SEGS * ST :]
    flags = jnp.concatenate([jnp.concatenate(masks, axis=0)] * KT, axis=1)
    factor = flags / (smooth * (1.0 / (2 * WF + 1)) + 1e-06)
    return (re * factor).astype(bf16).astype(f32), (im * factor).astype(bf16).astype(f32)


def spread(flags, g):
    return jnp.broadcast_to(flags[:, g : g + 1], (ST, 128))


def hour(ref):
    return [ref[h, :, 128 * i : 128 * (i + 1)].astype(f32) for h in range(2) for i in range(HALF // 128)]


def kernel(
    raw_hbm, mask_hbm, order_hbm, fir_hbm, box_hbm, dft_hbm, near_hbm, lag_hbm, out_ref,
    mask_ref, order_ref, fir_ref, box_ref, dft_ref, near_ref, lag_ref,
    own, own_mask, slots1, cand, slots2, picked, source, bulk,
    mslots1, mcand, mslots2, mpicked, source_mask, station, stack,
    copy_sem, pair_sem, mpair_sem, one_sem, two_sem, three_sem, mone_sem, mtwo_sem, mthree_sem,
):
    half = lax.axis_index("section")
    blk = lax.axis_index("blk")
    me = (blk // 16) * 2 + blk % 2
    x = (blk // 64) * 2 + half
    y = (blk // 16) % 4
    z = (blk // 2) % DEPTH
    core = blk % 2
    collects = x * y < 2
    late = x * y >= 2
    chip = x + y + 3 * ((y + 3) // 4) + 2 * x * y
    slot = jnp.where(collects, chip * 2 + core, PLANE)
    keeps_masks = half * N_BLK + blk == z * 2

    def device(chip, core):
        return (chip[0] % 2, (chip[0] // 2) * 64 + chip[1] * 16 + core + z * 2)

    collectors = [device(chip, i) for chip in CHIPS for i in range(2)]
    rest = [device(chip, i) for chip in REST for i in range(2)]

    def remote(src, dst, sems, to):
        return pltpu.make_async_remote_copy(
            src_ref=src, dst_ref=dst, send_sem=sems.at[0], recv_sem=sems.at[1],
            device_id=to, device_id_type=MESH,
        )

    def wait(ref, sem):
        pltpu.make_async_copy(ref, ref, sem).wait()

    def lanes(q):
        return pl.ds(q * PIECE if isinstance(q, int) else pl.multiple_of(q * PIECE, PIECE), PIECE)

    def above(depth):
        return (half, blk + (depth - z) * 2)

    other = (1 - half, blk)
    barrier = pltpu.get_barrier_semaphore()

    def signal(to):
        pl.semaphore_signal(barrier, inc=1, device_id=to, device_id_type=MESH)

    @pl.when(collects)
    def _():
        for to in rest:
            signal(to)

        for q, to in enumerate(collectors):

            @pl.when(slot != q)
            def _(to=to):
                signal(to)

        for depth in range(DEPTH):

            @pl.when(z != depth)
            def _(depth=depth):
                signal(above(depth))

    @pl.when(late)
    def _():
        signal(other)

    mine = own.at[half]
    copies = [
        pltpu.make_async_copy(src, dst, copy_sem.at[i])
        for i, (src, dst) in enumerate(
            (
                (raw_hbm, mine), (mask_hbm, mask_ref), (order_hbm, order_ref),
                (fir_hbm, fir_ref), (box_hbm, box_ref), (dft_hbm, dft_ref),
                (near_hbm, near_ref), (lag_hbm, lag_ref),
            )
        )
    ]
    for copy in copies:
        copy.start()
    copies[1].wait()
    flags = mask_ref[...].astype(f32)
    eye = lax.broadcasted_iota(jnp.int32, (ST, ST), 0) == lax.broadcasted_iota(
        jnp.int32, (ST, ST), 1
    )
    lane = lax.broadcasted_iota(jnp.int32, (ST, 128), 1)
    tile = jnp.zeros((ST, 128), f32)
    for g in range(SEG):
        row = jnp.where(eye, jnp.broadcast_to(flags[g : g + 1], (ST, ST)), 0.0)
        tile = jnp.where(lane == g, jnp.sum(row, axis=1, keepdims=True), tile)
    own_mask[half] = tile.astype(bf16)
    copies[0].wait()

    @pl.when(collects & (y < 2))
    def _():
        pl.semaphore_wait(barrier, DEPTH - 1 + PLANE - 1)

    @pl.when(collects & (y >= 2))
    def _():
        pl.semaphore_wait(barrier, DEPTH - 1 + PLANE)

    @pl.when(late & (x < 2))
    def _():
        pl.semaphore_wait(barrier, PLANE)

    @pl.when(late & (x >= 2))
    def _():
        pl.semaphore_wait(barrier, PLANE + 1)

    for q, to in enumerate(collectors):

        @pl.when(slot != q)
        def _(q=q, to=to):
            remote(own.at[half, :, lanes(q)], slots1.at[half, me], one_sem, to).start()

    pair = [
        remote(mine, mine, pair_sem, other),
        remote(own_mask.at[half], own_mask.at[half], mpair_sem, other),
    ]
    for copy in pair:
        copy.start()

    @pl.when(jnp.logical_not(keeps_masks))
    def _():
        remote(own_mask.at[half], mslots1.at[half, me], mone_sem, collectors[0]).start()

    copies[2].wait()
    root = [order_ref[i] for i in range(2)]
    root_plane = [(r // 16) * 2 + r % 2 for r in root]
    root_z = [(r // 2) % DEPTH for r in root]

    @pl.when(collects)
    def _():
        slots1[half, me] = own[half, :, lanes(slot)]
        wait(source.at[:, :, pl.ds(0, 31 * PIECE // 2)], one_sem.at[1])
        for i in range(2):
            for h in range(2):
                cand[i, h] = slots1[h, root_plane[i]]
        for depth in range(DEPTH):

            @pl.when(z != depth)
            def _(depth=depth):
                remote(cand, slots2.at[z], two_sem, above(depth)).start()

        slots2[z] = cand[...]

    @pl.when(keeps_masks)
    def _():
        mslots1[0, 0] = own_mask[0]
        wait(source.at[0, :, pl.ds(0, 31 * 128)], mone_sem.at[1])
        for i in range(2):
            for h in range(2):
                mcand[i, h] = mslots1[h, root_plane[i]]
        for depth in range(DEPTH):

            @pl.when(z != depth)
            def _(depth=depth):
                remote(mcand, mslots2.at[z], mtwo_sem, above(depth)).start()

        mslots2[z] = mcand[...]

    for copy in pair:
        copy.wait()
    for i in range(3, 7):
        copies[i].wait()
    weights = (fir_ref, box_ref, dft_ref, near_ref)
    masks = [own_mask[i].astype(f32) for i in range(2)]
    columns = [spread(m, g) for m in masks for g in range(SEG)]
    station[0], station[1] = whiten(hour(own), columns, *[w[...] for w in weights])

    @pl.when(collects)
    def _():
        wait(slots2.at[pl.ds(0, DEPTH - 1)], two_sem.at[1])
        for i in range(2):
            picked[i] = slots2[root_z[i], i]
        for q, to in enumerate(collectors):

            @pl.when(slot != q)
            def _(to=to):
                remote(picked.at[to[0]], source.at[:, :, lanes(slot)], three_sem, to).start()

        for to in rest:
            remote(picked.at[to[0]], source.at[:, :, lanes(slot)], three_sem, to).start()
        source[:, :, lanes(slot)] = picked[half]

    @pl.when(keeps_masks)
    def _():
        wait(mslots2.at[pl.ds(0, DEPTH - 1)], mtwo_sem.at[1])
        for i in range(2):
            mpicked[i] = mslots2[root_z[i], i]
        for to in collectors[1:] + rest:
            remote(mpicked.at[to[0]], source_mask, mthree_sem, to).start()
        source_mask[...] = mpicked[0]

    copies[7].wait()

    @pl.when(jnp.logical_not(keeps_masks))
    def _():
        wait(source_mask, mthree_sem.at[1])

    theirs = [source_mask[i].astype(f32) for i in range(2)]
    columns = [spread(m, g) for m in theirs for g in range(SEG)]
    shares = []
    for n in range(ST):
        count = masks[0] * theirs[0][n : n + 1] + masks[1] * theirs[1][n : n + 1]
        count = jnp.maximum(jnp.sum(count, axis=1, keepdims=True), 1.0)
        shares.append(jnp.broadcast_to(1.0 / count, (ST, 128)))

    @pl.when(collects)
    def _():
        wait(source.at[:, :, pl.ds(0, 15 * PIECE)], three_sem.at[1])

    @pl.when(late)
    def _():
        wait(source, three_sem.at[1])

    source_re, source_im = whiten(hour(source), columns, *[w[...] for w in weights])
    for k in range(KT):
        part = slice(128 * k, 128 * (k + 1))
        real = [jnp.zeros((ST, 128), f32)] * ST
        imag = [jnp.zeros((ST, 128), f32)] * ST
        for g in range(SEGS):
            re_s = station[0, ST * g : ST * (g + 1), part]
            im_s = station[1, ST * g : ST * (g + 1), part]
            for n in range(ST):
                re_n = source_re[ST * g + n : ST * g + n + 1, part]
                im_n = source_im[ST * g + n : ST * g + n + 1, part]
                real[n] = real[n] + (re_s * re_n + im_s * im_n)
                imag[n] = imag[n] + (im_s * re_n - re_s * im_n)
        for n in range(ST):
            stack[ST * n : ST * (n + 1), 128 * k : 128 * (k + 1)] = real[n]
            stack[ST * n : ST * (n + 1), NF + 128 * k : NF + 128 * (k + 1)] = imag[n]
    high, low = halves(stack[...])
    parts = dot(jnp.concatenate([high, low], axis=0), lag_ref[...])
    upper = parts[: ST * ST]
    lagged = upper[:, :LAGS] + upper[:, LAGS:] + parts[ST * ST :, :LAGS]
    for n in range(ST):
        share = jnp.concatenate([shares[n]] * (LAGS // 128), axis=1)
        out_ref[n] = lagged[ST * n : ST * (n + 1)] * share

    @pl.when(collects)
    def _():
        wait(source.at[0, :, pl.ds(0, 15 * PIECE)], one_sem.at[0])
        wait(slots2.at[pl.ds(0, DEPTH - 1)], two_sem.at[0])
        wait(bulk.at[pl.ds(0, 31)], three_sem.at[0])

    @pl.when(late)
    def _():
        wait(source.at[0], one_sem.at[0])

    @pl.when(keeps_masks)
    def _():
        wait(mslots2.at[pl.ds(0, DEPTH - 1)], mtwo_sem.at[0])
        wait(source.at[:, :, pl.ds(0, 31 * 128)], mthree_sem.at[0])

    @pl.when(jnp.logical_not(keeps_masks))
    def _():
        wait(own_mask.at[0], mone_sem.at[0])


def shards(raw_traces, valid_mask, block_order):
    constants = [jnp.asarray(t) for t in tables()]
    hbm = pl.BlockSpec(memory_space=pl.ANY)
    wide = (ST, PIECE)
    flag = (ST, 128)
    pair = pltpu.SemaphoreType.DMA((2,))
    return pl.pallas_call(
        kernel,
        out_shape=jax.ShapeDtypeStruct((ST, ST, LAGS), f32),
        in_specs=[hbm] * (3 + len(constants)),
        out_specs=pl.BlockSpec(memory_space=pltpu.VMEM),
        scratch_shapes=[
            pltpu.VMEM((SEG, ST), jnp.int32),
            pltpu.SMEM(block_order.shape, jnp.int32),
        ]
        + [pltpu.VMEM(c.shape, c.dtype) for c in constants]
        + [
            pltpu.VMEM((2, ST, HALF), bf16),
            pltpu.VMEM((2,) + flag, bf16),
            pltpu.VMEM((2, PLANE) + wide, bf16),
            pltpu.VMEM((2, 2) + wide, bf16),
            pltpu.VMEM((DEPTH, 2, 2) + wide, bf16),
            pltpu.VMEM((2, 2) + wide, bf16),
            pltpu.VMEM((2, ST, HALF), bf16),
            pltpu.VMEM((2 * PLANE, 2) + wide, bf16),
            pltpu.VMEM((2, PLANE) + flag, bf16),
            pltpu.VMEM((2, 2) + flag, bf16),
            pltpu.VMEM((DEPTH, 2, 2) + flag, bf16),
            pltpu.VMEM((2, 2) + flag, bf16),
            pltpu.VMEM((2,) + flag, bf16),
            pltpu.VMEM((2, SEGS * ST, NF), f32),
            pltpu.VMEM((ST * ST, 2 * NF), f32),
            pltpu.SemaphoreType.DMA((3 + len(constants),)),
            pair, pair, pair, pair, pair, pair, pair, pair,
        ],
        compiler_params=pltpu.CompilerParams(
            collective_id=0, has_side_effects=True, vmem_limit_bytes=VMEM_KIB << 10
        ),
    )(
        *[
            pltpu.with_memory_space_constraint(a, pltpu.HBM)
            for a in (raw_traces, valid_mask.T, block_order, *constants)
        ]
    )


def solution(mesh):
    return jax.shard_map(
        shards,
        mesh=mesh,
        in_specs=(P("blk", "section"), P("blk", "section"), P()),
        out_specs=P("section", "blk", None),
        check_vma=False,
    )
```
